512 devices in a mesh: dp: 32 (over z, core), expert: 16 (over y, x).
Axes of the slice: x: 4, y: 4, z: 16, core: 2. Of those that a mesh axis runs over, the one named last changes fastest.
Arguments:
- tokens: bfloat16 [65536, 2048], P(('dp', 'expert')), may hold values from -24 to 24
- queries: bfloat16 [65536, 128], P(('dp', 'expert')), may hold values from -4.5 to 4.5
- key_vectors: bfloat16 [65536, 128], P(('dp', 'expert')), may hold values from -4.5 to 4.5
- gate_logits: float32 [65536, 32], P(('dp', 'expert')), may hold values from -6 to 6
- value_routes: int32 [65536, 2], P(('dp', 'expert')), may hold values from 0 to 15, all different within a row; in each aligned block of 128 rows (0 to 127, 128 to 255, ...) at most 20 rows name the same one
- output_routes: int32 [65536, 2], P(('dp', 'expert')), may hold values from 0 to 15, all different within a row; in each aligned block of 128 rows (0 to 127, 128 to 255, ...) at most 20 rows name the same one
- value_weight: bfloat16 [16, 2048, 128], P('expert', 'dp'), may hold values from -0.125 to 0.125
- output_weight: bfloat16 [16, 2048, 128], P('expert', 'dp'), may hold values from -0.5 to 0.5
- cotangent: bfloat16 [65536, 2048], P(('dp', 'expert')), may hold values from -24 to 24
Outputs:
- token_grad: bfloat16 [65536, 2048], P(('dp', 'expert'))
- query_grad: bfloat16 [65536, 128], P(('dp', 'expert'))
- key_grad: bfloat16 [65536, 128], P(('dp', 'expert'))
- logit_grad: float32 [65536, 32], P(('dp', 'expert'))
- value_weight_grad: float32 [16, 2048, 128], P('expert', 'dp')
- output_weight_grad: float32 [16, 2048, 128], P('expert', 'dp')
The draws below stay inside these ranges and needn't reach their ends.
Inputs may be any that keep to these rules, and one draw needn't show every extreme that they name: `value_routes`: among one device's 128 tokens no value expert is named more than 20 times, a bound that some block reaches. `output_routes`: among one device's 128 tokens no output expert is named more than 20 times, a bound that some block reaches.
All inputs are finite; a program needn't handle non-finite values.
Results may differ from the reference program's by a relative error of at most 0.025.
Values may be sent and summed in bfloat16 or wider, within the bound.
A program may use at most 64 MiB of HBM per device.

```python
import math
import jax
import jax.numpy as jnp
import numpy as np
from jax import lax

D = 2048
HD = 128
TOK_DEV = 128
E = 16
CAP = 20
TOKENS = 65536
N_DP = 32


def attention_pair(key):
    base_query = jnp.clip(jax.random.normal(jax.random.fold_in(key, 101), (TOKENS, HD), jnp.float32), -4.5, 4.5)
    base_key = jnp.clip(jax.random.normal(jax.random.fold_in(key, 102), (TOKENS, HD), jnp.float32), -4.5, 4.5)
    return (base_query, base_key)


def draw_queries(key, part):
    return attention_pair(key)[0].astype(jnp.bfloat16)


def draw_key_vectors(key, part):
    return attention_pair(key)[1].astype(jnp.bfloat16)


def spiked(values, own_key, source, target, shards_of, factor):
    owner, partner = [(jnp.arange(values.shape[position]) // (values.shape[position] // shards_of)).reshape([-1 if axis == position else 1 for axis in range(values.ndim)]) for position in (source, target)]
    chosen = jax.random.permutation(own_key, shards_of)[partner]
    strong = (owner == chosen) | (owner == (partner + shards_of // 2) % shards_of)
    return jnp.where(strong, factor * values, values)


def levels(key, extent, pieces, least, largest):
    level = 1.0
    for dim, shards_of in pieces:
        heights = jax.random.uniform(jax.random.fold_in(jax.random.fold_in(key, 6), dim), (shards_of,), jnp.float32, least / len(pieces), largest / len(pieces))
        level = level * jnp.repeat(jnp.exp(heights), extent[dim] // shards_of).reshape((-1,) + (1,) * (len(extent) - 1 - dim))
    return level


def assign_block(key, own, number, rows, number_of, top, bound, lean):
    ranking = jax.random.permutation(key, number_of)
    heavy_load, common = load_shares(number_of, rows * top, bound, lean, True), load_shares(number_of, rows * top, bound, lean, False)
    places = jnp.arange(number_of)

    def named(sizes, rotation):
        used = int((sizes > 0).sum())
        fixed = max(1, used // 4)
        shifted = fixed + (places - fixed + rotation * (used - fixed)) % max(1, number_of - fixed)
        return jnp.zeros((number_of,), jnp.int32).at[ranking[jnp.where(places < fixed, places, shifted)]].set(jnp.asarray(sizes, jnp.int32))

    sizes = jnp.where(number % 4 == 0, named(heavy_load, number // 4), named(common, number - number // 4 - 1))
    mixed = jax.random.permutation(jax.random.fold_in(own, 3), number_of)
    source_of, sink = mixed[0:number_of // 2 * 2:2], mixed[1:number_of // 2 * 2:2]
    slack = jnp.minimum(sizes[source_of] - 1, bound - sizes[sink]) // 2
    slack = jnp.where((source_of == ranking[0]) | (sink == ranking[0]) | (sizes[sink] == 0), 0, jnp.maximum(slack, 0))
    shifted = jax.random.randint(jax.random.fold_in(own, 4), (number_of // 2,), 0, 1 << 20) % (slack + 1)
    sizes = sizes.at[source_of].add(-shifted).at[sink].add(shifted)
    labels = jnp.searchsorted(jnp.cumsum(sizes), jnp.arange(rows * top), side="right").astype(jnp.int32)
    grid = labels.reshape(top, rows).T
    grid = grid[jax.random.permutation(jax.random.fold_in(own, 1), rows)]
    rotation = jax.random.randint(jax.random.fold_in(own, 2), (rows, 1), 0, top)
    return jnp.take_along_axis(grid, (jnp.arange(top)[None, :] + rotation) % top, axis=1)


def load_shares(number_of, total, reach, slope, full):
    loads = [(1 << 20) // math.isqrt(standing ** slope) + 1 for standing in range(1, number_of + 1)]
    largest = reach if full else min(reach, max(-(-total // number_of), total * loads[0] // sum(loads)))
    least = 1 if total - largest >= number_of - 1 else 0
    counts, rest = [largest] + [least] * (number_of - 1), total - largest - least * (number_of - 1)
    while rest > 0:
        candidates = [i for i in range(1, number_of) if counts[i] < largest] or [i for i in range(1, number_of) if counts[i] < reach]
        pool, left = sum([loads[i] for i in candidates]), rest
        for i in candidates:
            extra = min(reach - counts[i], max(1, left * loads[i] // pool), rest)
            counts[i] = counts[i] + extra
            rest = rest - extra
    return np.array(counts)


def gaussian(own_key, extent, deviation, limit, cuts=(), kind=jnp.bfloat16):
    values = deviation * jax.random.normal(own_key, extent, jnp.float32)
    if cuts:
        values = values * levels(own_key, extent, cuts, -0.22, 0.18)
    return jnp.clip(values, -limit, limit).astype(kind)


def noise_with(rng, shape, width, limit, shards, heavy, held_as=jnp.bfloat16):
    result = width * jax.random.normal(rng, shape, jnp.float32)
    if shards:
        result = result * levels(rng, shape, shards, -0.22, 0.18)
    return jnp.clip(spiked(result, jax.random.fold_in(rng, 3), *heavy), -limit, limit).astype(held_as)


def setup_inputs(seed: int = 0) -> dict:
    keys = jax.random.split(jax.random.key(seed), 10)
    tokens = noise_with(keys[0], (TOKENS, D), 1.0, 24.0, ((0, 512),), (0, 1, 512, 6.0))
    queries = draw_queries(jax.random.fold_in(keys[9], 71), 0)
    key_vectors = draw_key_vectors(jax.random.fold_in(keys[9], 71), 0)
    gate_logits = gaussian(keys[3], (TOKENS, 2 * E), 1.5, 6.0, ((0, 512),), jnp.float32)
    value_routes_keys = jax.random.split(jax.random.fold_in(keys[4], 1), TOKENS // TOK_DEV)
    value_routes_turns = jax.random.permutation(jax.random.fold_in(keys[4], 3), TOKENS // TOK_DEV)
    value_routes = jax.vmap(lambda own, number: assign_block(jax.random.fold_in(keys[4], 2), own, number, TOK_DEV, E, 2, CAP, 2))(value_routes_keys, value_routes_turns).reshape((TOKENS, 2))
    output_routes_keys = jax.random.split(jax.random.fold_in(keys[5], 1), TOKENS // TOK_DEV)
    output_routes_turns = jax.random.permutation(jax.random.fold_in(keys[5], 3), TOKENS // TOK_DEV)
    output_routes = jax.vmap(lambda own, number: assign_block(jax.random.fold_in(keys[5], 2), own, number, TOK_DEV, E, 2, CAP, 2))(output_routes_keys, output_routes_turns).reshape((TOKENS, 2))
    value_weight = gaussian(keys[6], (E, D, HD), D ** -0.5, 0.125, ((0, 16), (1, 32)))
    output_weight = gaussian(keys[7], (E, D, HD), HD ** -0.5, 0.5, ((0, 16), (1, 32)))
    cotangent = noise_with(keys[8], (TOKENS, D), 1.0, 24.0, ((0, 512),), (0, 1, 512, 6.0))
    return {"tokens": tokens, "queries": queries, "key_vectors": key_vectors, "gate_logits": gate_logits, "value_routes": value_routes, "output_routes": output_routes, "value_weight": value_weight, "output_weight": output_weight, "cotangent": cotangent}


def slot_index(routes, experts, capacity):
    flattened = routes.reshape(-1)
    onehot = (flattened[:, None] == jnp.arange(experts, dtype=jnp.int32)[None, :]).astype(jnp.int32)
    before = jnp.cumsum(onehot, axis=0) - onehot
    return (flattened * capacity + lax.optimization_barrier(jnp.sum(before * onehot, axis=1))).astype(jnp.int32)

def owner_rows(slots, experts, capacity):
    row_count = slots.shape[0]
    owner_table = jnp.full((experts * capacity,), row_count, jnp.int32)
    return owner_table.at[slots].set(jnp.arange(row_count, dtype=jnp.int32))

def causal_probs(queries, key_vectors):
    length_rows = queries.shape[0]
    scores = jnp.dot(queries, key_vectors.T, preferred_element_type=jnp.float32) / math.sqrt(queries.shape[1])
    row_ids = lax.broadcasted_iota(jnp.int32, (length_rows, length_rows), 0)
    col_ids = lax.broadcasted_iota(jnp.int32, (length_rows, length_rows), 1)
    scores = jnp.where(row_ids >= col_ids, scores, -1e+30)
    row_max = lax.optimization_barrier(jnp.max(scores, axis=1, keepdims=True))
    exponent = jnp.exp(scores - row_max)
    return exponent / lax.optimization_barrier(jnp.sum(exponent, axis=1, keepdims=True))

def attend(packed):
    probs = causal_probs(packed[0], packed[1])
    weights = probs.astype(jnp.bfloat16)
    return jnp.dot(weights, packed[2], preferred_element_type=jnp.float32).astype(jnp.bfloat16)

def attend_back(packed):
    queries, key_vectors, mixed_value, hidden_grad = packed
    probs = causal_probs(queries, key_vectors)
    weights = probs.astype(jnp.bfloat16)
    prob_grad = jnp.dot(hidden_grad, mixed_value.T, preferred_element_type=jnp.float32)
    score_grad = probs * (prob_grad - lax.optimization_barrier(jnp.sum(prob_grad * probs, axis=1, keepdims=True)))
    scaled_grad = (score_grad / math.sqrt(queries.shape[1])).astype(jnp.bfloat16)
    query_grad = jnp.dot(scaled_grad, key_vectors, preferred_element_type=jnp.float32).astype(jnp.bfloat16)
    key_grad = jnp.dot(scaled_grad.T, queries, preferred_element_type=jnp.float32).astype(jnp.bfloat16)
    value_grad = jnp.dot(weights.T, hidden_grad, preferred_element_type=jnp.float32).astype(jnp.bfloat16)
    return (query_grad, key_grad, value_grad)

def group_sum(row_block, other_rows):
    partials = jnp.einsum('gnd,gnh->gdh', row_block.reshape(N_DP, -1, D).astype(jnp.float32), other_rows.reshape(N_DP, -1, HD).astype(jnp.float32))
    rounded = lax.optimization_barrier(partials.astype(jnp.bfloat16))
    return lax.optimization_barrier(jnp.sum(rounded.astype(jnp.float32), axis=0)) / N_DP

def reference(tokens, queries, key_vectors, gate_logits, value_routes, output_routes, value_weight, output_weight, cotangent):
    capacity = 5 * TOK_DEV // (2 * E)
    blocks = TOKENS // TOK_DEV
    pair_count = 2 * TOK_DEV
    gate_values = jax.nn.sigmoid(gate_logits)
    value_gate = jnp.take_along_axis(gate_values[:, :E], value_routes, axis=1)
    output_gate = jnp.take_along_axis(gate_values[:, E:], output_routes, axis=1)

    def block_slots(routes):
        return slot_index(routes, E, capacity)

    def block_owners(slots):
        return owner_rows(slots, E, capacity)
    slot_value = jax.vmap(block_slots)(value_routes.reshape(blocks, TOK_DEV, 2))
    slot_output = jax.vmap(block_slots)(output_routes.reshape(blocks, TOK_DEV, 2))

    def expert_index(owners):
        block_start = jnp.arange(blocks, dtype=jnp.int32)[:, None]
        token_index = jnp.where(owners < pair_count, block_start * TOK_DEV + owners // 2, TOKENS).astype(jnp.int32)
        pair_index = jnp.where(owners < pair_count, block_start * pair_count + owners, 2 * TOKENS).astype(jnp.int32)
        token_index = token_index.reshape(blocks, E, capacity).transpose(1, 0, 2).reshape(E, blocks * capacity)
        pair_index = pair_index.reshape(blocks, E, capacity).transpose(1, 0, 2).reshape(E, blocks * capacity)
        return (token_index, pair_index)
    token_value, pair_value = expert_index(jax.vmap(block_owners)(slot_value))
    token_output, pair_output = expert_index(jax.vmap(block_owners)(slot_output))

    def per_slot(results, slots):
        row_width = results.shape[-1]
        slot_grid = results.reshape(E, blocks, capacity, row_width).transpose(1, 0, 2, 3).reshape(blocks, E * capacity, row_width)

        def pick_rows(grid_block, slot_block):
            return grid_block[slot_block]
        return jax.vmap(pick_rows)(slot_grid, slots).reshape(TOKENS, 2, row_width)

    def value_expert(packed):
        row_block = jnp.take(tokens, packed[0], axis=0, mode='fill', fill_value=0)
        return jnp.dot(row_block, packed[1], preferred_element_type=jnp.float32).astype(jnp.bfloat16)
    expert_value = per_slot(lax.map(value_expert, (token_value, value_weight)), slot_value).astype(jnp.float32)
    mixed_value = lax.optimization_barrier(jnp.sum(value_gate[:, :, None] * expert_value, axis=1)).astype(jnp.bfloat16)

    def by_sequence(array):
        return array.reshape(blocks, TOK_DEV, array.shape[-1])
    hidden = lax.map(attend, (by_sequence(queries), by_sequence(key_vectors), by_sequence(mixed_value))).reshape(TOKENS, HD)
    gated_hidden = (output_gate[:, :, None] * hidden[:, None, :].astype(jnp.float32)).astype(jnp.bfloat16).reshape(2 * TOKENS, HD)

    def output_expert(packed):
        row_block = jnp.take(cotangent, packed[0], axis=0, mode='fill', fill_value=0)
        gated_rows = jnp.take(gated_hidden, packed[1], axis=0, mode='fill', fill_value=0)
        returned = jnp.dot(row_block, packed[2], preferred_element_type=jnp.float32).astype(jnp.bfloat16)
        return (returned, group_sum(row_block, gated_rows))
    head_rows, output_weight_grad = lax.map(output_expert, (token_output, pair_output, output_weight))
    head_back = per_slot(head_rows, slot_output).astype(jnp.float32)
    output_gate_grad = lax.optimization_barrier(jnp.sum(hidden[:, None, :].astype(jnp.float32) * head_back, axis=2))
    hidden_grad = lax.optimization_barrier(jnp.sum(output_gate[:, :, None] * head_back, axis=1)).astype(jnp.bfloat16)
    query_grad, key_grad, value_grad = lax.map(attend_back, (by_sequence(queries), by_sequence(key_vectors), by_sequence(mixed_value), by_sequence(hidden_grad)))
    query_grad = query_grad.reshape(TOKENS, HD)
    key_grad = key_grad.reshape(TOKENS, HD)
    value_grad = value_grad.reshape(TOKENS, HD)
    gated_value = (value_gate[:, :, None] * value_grad[:, None, :].astype(jnp.float32)).astype(jnp.bfloat16).reshape(2 * TOKENS, HD)
    value_gate_grad = lax.optimization_barrier(jnp.sum(value_grad[:, None, :].astype(jnp.float32) * expert_value, axis=2))

    def value_backward(running, packed):
        row_block = jnp.take(tokens, packed[0], axis=0, mode='fill', fill_value=0)
        gated_rows = jnp.take(gated_value, packed[1], axis=0, mode='fill', fill_value=0)
        returned = lax.dot_general(gated_rows, packed[2], (((1,), (1,)), ((), ())), preferred_element_type=jnp.float32).astype(jnp.bfloat16)
        running = running.at[packed[0]].add(returned.astype(jnp.float32), mode='drop')
        return (running, group_sum(row_block, gated_rows))
    summed, value_weight_grad = lax.scan(value_backward, jnp.zeros((TOKENS, D), jnp.float32), (token_value, pair_value, value_weight))
    token_grad = summed.astype(jnp.bfloat16)
    expert_ids = jnp.arange(E, dtype=jnp.int32)[None, None, :]
    hot_value = (value_routes[:, :, None] == expert_ids).astype(jnp.float32)
    hot_output = (output_routes[:, :, None] == expert_ids).astype(jnp.float32)
    logit_value = lax.optimization_barrier(jnp.sum(hot_value * (value_gate_grad * value_gate * (1.0 - value_gate))[:, :, None], axis=1))
    logit_output = lax.optimization_barrier(jnp.sum(hot_output * (output_gate_grad * output_gate * (1.0 - output_gate))[:, :, None], axis=1))
    logit_grad = jnp.concatenate([logit_value, logit_output], axis=1)
    return (token_grad, query_grad, key_grad, logit_grad, value_weight_grad, output_weight_grad)
```

```python
import math

import jax
import jax.numpy as jnp
from jax import lax
from jax.sharding import PartitionSpec as P

BF16 = jnp.bfloat16
F32 = jnp.float32


def contract(left, right, dims):
    return lax.dot_general(left, right, (dims, ((), ())), preferred_element_type=F32)


def route_picks(routes, experts, stride, offset, width):
    rows = routes.shape[0]
    expert_ids = lax.broadcasted_iota(jnp.int32, (rows, experts), 1)
    hots = [(expert_ids == routes[:, k : k + 1]).astype(F32) for k in range(2)]
    row_ids = lax.broadcasted_iota(jnp.int32, (rows, rows), 0)
    col_ids = lax.broadcasted_iota(jnp.int32, (rows, rows), 1)
    earlier = (col_ids < row_ids).astype(BF16)
    rank = contract(earlier, (hots[0] + hots[1]).astype(BF16), ((1,), (0,)))
    place = rank + (expert_ids * stride + offset).astype(F32)
    slot_ids = lax.broadcasted_iota(jnp.int32, (rows, width), 1)
    picks = [
        (slot_ids == jnp.sum(hot * place, axis=1, keepdims=True).astype(jnp.int32)) for hot in hots
    ]
    return hots, [pick.astype(BF16) for pick in picks]


def attention_step(queries, keys, gate_logits, returned, value_hot, output_hot, value_pick, output_pick):
    rows, head_size = queries.shape
    experts = gate_logits.shape[1] // 2
    gates = jax.nn.sigmoid(gate_logits)
    value_gate = [jnp.sum(hot * gates[:, :experts], axis=1, keepdims=True) for hot in value_hot]
    output_gate = [jnp.sum(hot * gates[:, experts:], axis=1, keepdims=True) for hot in output_hot]
    expert_value = [contract(pick, returned, ((1,), (0,))) for pick in value_pick]
    head_back = [contract(pick, returned, ((1,), (0,))) for pick in output_pick]
    mixed_value = (value_gate[0] * expert_value[0] + value_gate[1] * expert_value[1]).astype(BF16)
    scores = contract(queries, keys, ((1,), (1,))) / math.sqrt(head_size)
    row_ids = lax.broadcasted_iota(jnp.int32, (rows, rows), 0)
    col_ids = lax.broadcasted_iota(jnp.int32, (rows, rows), 1)
    scores = jnp.where(row_ids >= col_ids, scores, -1e30)
    exponent = jnp.exp(scores - jnp.max(scores, axis=1, keepdims=True))
    probs = exponent / jnp.sum(exponent, axis=1, keepdims=True)
    weights = probs.astype(BF16)
    hidden = contract(weights, mixed_value, ((1,), (0,))).astype(BF16)
    hidden_wide = hidden.astype(F32)
    hidden_grad = (output_gate[0] * head_back[0] + output_gate[1] * head_back[1]).astype(BF16)
    prob_grad = contract(hidden_grad, mixed_value, ((1,), (1,)))
    score_grad = probs * (prob_grad - jnp.sum(prob_grad * probs, axis=1, keepdims=True))
    scaled_grad = (score_grad / math.sqrt(head_size)).astype(BF16)
    query_grad = contract(scaled_grad, keys, ((1,), (0,))).astype(BF16)
    key_grad = contract(scaled_grad, queries, ((0,), (0,))).astype(BF16)
    value_grad = contract(weights, hidden_grad, ((0,), (0,))).astype(BF16)
    value_wide = value_grad.astype(F32)
    gated_value = [(gate * value_wide).astype(BF16) for gate in value_gate]
    gated_hidden = [(gate * hidden_wide).astype(BF16) for gate in output_gate]
    logit_value = 0.0
    logit_output = 0.0
    for k in range(2):
        slope = jnp.sum(value_wide * expert_value[k], axis=1, keepdims=True)
        logit_value += value_hot[k] * (slope * value_gate[k] * (1.0 - value_gate[k]))
        slope = jnp.sum(hidden_wide * head_back[k], axis=1, keepdims=True)
        logit_output += output_hot[k] * (slope * output_gate[k] * (1.0 - output_gate[k]))
    logit_grad = jnp.concatenate([logit_value, logit_output], axis=1)
    sent_rows = contract(
        jnp.concatenate(value_pick + output_pick, axis=0),
        jnp.concatenate(gated_value + gated_hidden, axis=0),
        ((0,), (0,)),
    ).astype(BF16)
    return query_grad, key_grad, logit_grad, sent_rows


def exchange(rows, axis, count):
    blocks = rows.reshape(count, rows.shape[0] // count, rows.shape[1])
    return lax.all_to_all(blocks, axis, split_axis=0, concat_axis=0, tiled=True).reshape(rows.shape)


def on_device(
    tokens,
    queries,
    key_vectors,
    gate_logits,
    value_routes,
    output_routes,
    value_weight,
    output_weight,
    cotangent,
):
    tok_rows, features = tokens.shape
    head_size = queries.shape[1]
    experts = gate_logits.shape[1] // 2
    capacity = 5 * tok_rows // (2 * experts)
    stride = 2 * capacity
    slots = experts * stride
    groups = lax.axis_size("dp")
    half = features // 2
    shard = jnp.concatenate([value_weight[0], output_weight[0]], axis=1)
    banks = exchange(
        jnp.broadcast_to(shard[None], (groups,) + shard.shape).reshape(features, 2 * head_size), "dp", groups
    )
    value_hot, value_pick = route_picks(value_routes, experts, stride, 0, slots)
    output_hot, output_pick = route_picks(output_routes, experts, stride, capacity, slots)
    sent = contract(
        jnp.concatenate([value_pick[0] + value_pick[1], output_pick[0] + output_pick[1]], axis=0),
        jnp.concatenate([tokens, cotangent], axis=0),
        ((0,), (0,)),
    ).astype(BF16)
    held = exchange(sent, "expert", experts)
    slot_ids = lax.broadcasted_iota(jnp.int32, (slots, 1), 0) % stride
    is_value = slot_ids < capacity
    both = contract(held, banks, ((1,), (0,)))
    answer = jnp.where(is_value, both[:, :head_size], both[:, head_size:]).astype(BF16)
    returned = exchange(answer, "expert", experts)
    query_grad, key_grad, logit_grad, sent_rows = attention_step(
        queries, key_vectors, gate_logits, returned, value_hot, output_hot, value_pick, output_pick
    )
    held_rows = exchange(sent_rows, "expert", experts)
    zero = jnp.zeros_like(held_rows)
    wide_rows = jnp.concatenate(
        [jnp.where(is_value, held_rows, zero), jnp.where(is_value, zero, held_rows)], axis=1
    )
    partial = contract(held, wide_rows, ((0,), (0,))).astype(BF16)
    summed = exchange(partial, "dp", groups).reshape(groups, features // groups, 2 * head_size)
    summed = jnp.sum(summed.astype(F32), axis=0) / groups
    value_rows = held_rows.reshape(experts, stride, head_size)[:, :capacity]
    blank = jnp.zeros_like(value_rows)
    halves = jnp.concatenate(
        [jnp.concatenate([value_rows, blank], axis=1), jnp.concatenate([blank, value_rows], axis=1)], axis=2
    ).reshape(slots, 2 * head_size)
    half_banks = jnp.concatenate([banks[:half, :head_size], banks[half:, :head_size]], axis=1)
    back = contract(halves, half_banks, ((1,), (1,))).astype(BF16)
    back = exchange(back, "expert", experts)
    pick_low = value_pick[0] + value_pick[1]
    pick_high = jnp.concatenate([jnp.zeros((tok_rows, capacity), BF16), pick_low[:, :-capacity]], axis=1)
    token_grad = jnp.concatenate(
        [contract(pick, back, ((1,), (0,))).astype(BF16) for pick in (pick_low, pick_high)], axis=1
    )
    return (
        token_grad,
        query_grad,
        key_grad,
        logit_grad,
        summed[None, :, :head_size],
        summed[None, :, head_size:],
    )


def solution(mesh):
    rows = P(("dp", "expert"), None)
    bank = P("expert", "dp", None)
    return jax.shard_map(
        on_device,
        mesh=mesh,
        in_specs=(rows,) * 6 + (bank, bank, rows),
        out_specs=(rows,) * 4 + (bank, bank),
        check_vma=False,
    )
```

```python
import functools
import math

import jax
import jax.numpy as jnp
from jax import lax
from jax.experimental import pallas as pl
from jax.experimental.pallas import tpu as pltpu
from jax.sharding import PartitionSpec as P

BF16 = jnp.bfloat16
F32 = jnp.float32
MESH = pl.DeviceIdType.MESH
SIDE = 4


def contract(left, right, dims):
    return lax.dot_general(left, right, (dims, ((), ())), preferred_element_type=F32)


def route_ranks(routes, experts):
    rows = routes.shape[0]
    expert_ids = lax.broadcasted_iota(jnp.int32, (rows, experts), 1)
    hots = [jnp.where(expert_ids == routes[:, k : k + 1], 1.0, 0.0).astype(F32) for k in range(2)]
    row_ids = lax.broadcasted_iota(jnp.int32, (rows, rows), 0)
    col_ids = lax.broadcasted_iota(jnp.int32, (rows, rows), 1)
    earlier = jnp.where(col_ids < row_ids, 1.0, 0.0).astype(BF16)
    rank = contract(earlier, (hots[0] + hots[1]).astype(BF16), ((1,), (0,)))
    places = [jnp.sum(hot * rank, axis=1, keepdims=True).astype(jnp.int32) for hot in hots]
    return hots, [routes[:, k : k + 1] for k in range(2)], places


def pick_rows(expert, place, stride, offset, width):
    slot_ids = lax.broadcasted_iota(jnp.int32, (expert.shape[0], width), 1)
    return jnp.where(slot_ids == expert * stride + place + offset, 1.0, 0.0).astype(F32)


def attention_step(queries, keys, gate_logits, returned, value_hot, output_hot, value_pick, output_pick):
    rows, head_size = queries.shape
    experts = gate_logits.shape[1] // 2
    gates = jax.nn.sigmoid(gate_logits)
    value_gate = [jnp.sum(hot * gates[:, :experts], axis=1, keepdims=True) for hot in value_hot]
    output_gate = [jnp.sum(hot * gates[:, experts:], axis=1, keepdims=True) for hot in output_hot]
    expert_value = [contract(pick, returned, ((1,), (0,))) for pick in value_pick]
    head_back = [contract(pick, returned, ((1,), (0,))) for pick in output_pick]
    mixed_value = (value_gate[0] * expert_value[0] + value_gate[1] * expert_value[1]).astype(BF16)
    scores = contract(queries, keys, ((1,), (1,))) / math.sqrt(head_size)
    row_ids = lax.broadcasted_iota(jnp.int32, (rows, rows), 0)
    col_ids = lax.broadcasted_iota(jnp.int32, (rows, rows), 1)
    scores = jnp.where(row_ids >= col_ids, scores, -1e30)
    exponent = jnp.exp(scores - jnp.max(scores, axis=1, keepdims=True))
    probs = exponent / jnp.sum(exponent, axis=1, keepdims=True)
    weights = probs.astype(BF16)
    hidden = contract(weights, mixed_value, ((1,), (0,))).astype(BF16)
    hidden_wide = hidden.astype(F32)
    hidden_grad = (output_gate[0] * head_back[0] + output_gate[1] * head_back[1]).astype(BF16)
    prob_grad = contract(hidden_grad, mixed_value, ((1,), (1,)))
    score_grad = probs * (prob_grad - jnp.sum(prob_grad * probs, axis=1, keepdims=True))
    scaled_grad = (score_grad / math.sqrt(head_size)).astype(BF16)
    query_grad = contract(scaled_grad, keys, ((1,), (0,))).astype(BF16)
    key_grad = contract(scaled_grad, queries, ((0,), (0,))).astype(BF16)
    value_grad = contract(weights, hidden_grad, ((0,), (0,))).astype(BF16)
    value_wide = value_grad.astype(F32)
    gated_value = [(gate * value_wide).astype(BF16) for gate in value_gate]
    gated_hidden = [(gate * hidden_wide).astype(BF16) for gate in output_gate]
    logit_value = 0.0
    logit_output = 0.0
    for k in range(2):
        slope = jnp.sum(value_wide * expert_value[k], axis=1, keepdims=True)
        logit_value += value_hot[k] * (slope * value_gate[k] * (1.0 - value_gate[k]))
        slope = jnp.sum(hidden_wide * head_back[k], axis=1, keepdims=True)
        logit_output += output_hot[k] * (slope * output_gate[k] * (1.0 - output_gate[k]))
    logit_grad = jnp.concatenate([logit_value, logit_output], axis=1)
    sent_rows = contract(
        jnp.concatenate(value_pick + output_pick, axis=0),
        jnp.concatenate(gated_value + gated_hidden, axis=0),
        ((0,), (0,)),
    ).astype(BF16)
    return query_grad, key_grad, logit_grad, sent_rows


def kernel(
    groups,
    tokens,
    queries,
    key_vectors,
    gate_logits,
    value_routes,
    output_routes,
    shard,
    cotangent,
    token_grad,
    query_grad,
    key_grad,
    logit_grad,
    value_weight_grad,
    output_weight_grad,
    sent,
    held,
    banks,
    quarter_bank,
    answer,
    returned,
    gated,
    held_rows,
    wide,
    spread,
    parts,
    pair,
    staged,
    landed,
    back,
    back_in,
    send_x,
    recv_x,
    send_z,
    recv_z,
    send_f,
    recv_f,
    send_p,
    recv_p,
    local,
):
    tok_rows, features = tokens.shape
    head_size = queries.shape[1]
    experts = gate_logits.shape[1] // 2
    capacity = 5 * tok_rows // (2 * experts)
    half, quarter = features // 2, features // 4
    chips = groups // 2
    shard_rows = features // groups
    block = 4 * capacity
    small = answer.shape[0] // experts
    me_dp = lax.axis_index("dp")
    me_ex = lax.axis_index("expert")
    z, core = me_dp // 2, me_dp % 2
    y, x = me_ex // SIDE, me_ex % SIDE
    partner = z * 2 + 1 - core

    def plane_peer(i):
        return ((y + i // SIDE) % SIDE) * SIDE + (x + i % SIDE) % SIDE

    def chip_step(j):
        return (j % 2) * ((j + 1) // 2) + (1 - j % 2) * (chips - j // 2)

    def chip_peer(j):
        return ((z + chip_step(j)) % chips) * 2 + core

    def chip_source(j):
        return ((z + chips - chip_step(j)) % chips) * 2 + core

    def window(ref, index, size):
        return ref.at[pl.ds(pl.multiple_of(index * size, 16), size)]

    def plane_copy(phase, source, target, size, i):
        peer = plane_peer(i)
        return pltpu.make_async_remote_copy(
            src_ref=window(source, peer, size),
            dst_ref=window(target, me_ex, size),
            send_sem=send_x.at[phase, i],
            recv_sem=recv_x.at[phase, i],
            device_id={"expert": peer},
            device_id_type=MESH,
        )

    def plane_own(phase, source, target, size):
        return pltpu.make_async_copy(
            window(source, me_ex, size), window(target, me_ex, size), local.at[phase]
        )

    def plane_start(phase, source, target, size):
        @pl.loop(1, experts)
        def _(i):
            plane_copy(phase, source, target, size, i).start()

        plane_own(phase, source, target, size).start()

    def plane_wait(phase, source, target, size):
        plane_own(phase, source, target, size).wait()

        @pl.loop(1, experts)
        def _(i):
            plane_copy(phase, source, target, size, i).wait_recv()

    def plane_drain(phase, source, target, size):
        @pl.loop(1, experts)
        def _(i):
            plane_copy(phase, source, target, size, i).wait_send()

    def shard_copy(j):
        return pltpu.make_async_remote_copy(
            src_ref=shard,
            dst_ref=window(banks, me_dp, shard_rows),
            send_sem=send_z.at[0, j],
            recv_sem=recv_z.at[0, j],
            device_id={"dp": chip_peer(j)},
            device_id_type=MESH,
        )

    def forward_copy(j, source, row):
        return pltpu.make_async_remote_copy(
            src_ref=source,
            dst_ref=window(banks, row, shard_rows),
            send_sem=send_f.at[j],
            recv_sem=recv_f.at[j],
            device_id={"dp": partner},
            device_id_type=MESH,
        )

    def forward_of(j):
        row = chip_source(j)
        return forward_copy(j, window(banks, row, shard_rows), row)

    def sum_copy(j):
        return pltpu.make_async_remote_copy(
            src_ref=staged.at[(z + chip_step(j)) % chips],
            dst_ref=landed.at[z],
            send_sem=send_z.at[1, j],
            recv_sem=recv_z.at[1, j],
            device_id={"dp": chip_peer(j)},
            device_id_type=MESH,
        )

    pair_copy = pltpu.make_async_remote_copy(
        src_ref=parts.at[1 - core],
        dst_ref=pair,
        send_sem=send_p,
        recv_sem=recv_p,
        device_id={"dp": partner},
        device_id_type=MESH,
    )

    barrier = pltpu.get_barrier_semaphore()

    @pl.loop(1, experts)
    def _(i):
        pl.semaphore_signal(barrier, inc=1, device_id={"expert": plane_peer(i)}, device_id_type=MESH)

    @pl.loop(1, chips)
    def _(j):
        pl.semaphore_signal(barrier, inc=1, device_id={"dp": chip_peer(j)}, device_id_type=MESH)

    pl.semaphore_signal(barrier, inc=1, device_id={"dp": partner}, device_id_type=MESH)

    own_shard = pltpu.make_async_copy(shard, window(banks, me_dp, shard_rows), local.at[4])
    own_shard.start()
    value_hot, value_expert, value_place = route_ranks(value_routes[...], experts)
    output_hot, output_expert, output_place = route_ranks(output_routes[...], experts)

    def pick_sum(expert, place, stride, offset, width):
        picks = [pick_rows(expert[k], place[k], stride, offset, width) for k in range(2)]
        return (picks[0] + picks[1]).astype(BF16)

    width = experts * block
    chosen = jnp.concatenate(
        [
            pick_sum(expert, place, block, offset, width)
            for expert, place, offset in (
                (value_expert, value_place, 0),
                (output_expert, output_place, capacity),
                (value_expert, value_place, 2 * capacity),
                (output_expert, output_place, 3 * capacity),
            )
        ],
        axis=0,
    )
    tile = 256
    cut = width // 2
    for c in range(half // tile):
        low = pl.ds(c * tile, tile)
        high = pl.ds(half + c * tile, tile)
        rows = jnp.concatenate([tokens[:, low], cotangent[:, low], tokens[:, high], cotangent[:, high]], axis=0)
        for part in range(2):
            sent[part * cut : (part + 1) * cut, low] = contract(
                chosen[:, part * cut : (part + 1) * cut], rows, ((0,), (0,))
            ).astype(BF16)

    pl.semaphore_wait(barrier, experts - 1 + chips)

    @pl.loop(1, chips)
    def _(j):
        shard_copy(j).start()

    plane_start(0, sent, held, block)
    forward_copy(0, shard, me_dp).start()

    @pl.loop(1, chips)
    def _(j):
        shard_copy(j).wait_recv()
        forward_of(j).start()

    own_shard.wait()

    @pl.loop(0, chips)
    def _(j):
        forward_of(j).wait_recv()

    bank_pair = jnp.concatenate([banks[:half, :], banks[half:, :]], axis=1)
    for q in range(4):
        quarter_bank[:, q * head_size : (q + 1) * head_size] = banks[q * quarter : (q + 1) * quarter, :head_size]

    plane_wait(0, sent, held, block)

    row_ids = lax.broadcasted_iota(jnp.int32, (2 * capacity, head_size), 0)
    chunk = 4
    for c in range(experts // chunk):
        both = contract(held[c * chunk * block : (c + 1) * chunk * block, :], bank_pair, ((1,), (0,)))
        for k in range(chunk):
            top = both[k * block : k * block + 2 * capacity, : 2 * head_size]
            low = both[k * block + 2 * capacity : (k + 1) * block, 2 * head_size :]
            total = top + low
            rows = jnp.where(row_ids < capacity, total[:, :head_size], total[:, head_size:])
            rows = jnp.concatenate([rows, jnp.zeros((small - 2 * capacity, head_size), F32)], axis=0)
            e = c * chunk + k
            answer[e * small : (e + 1) * small, :] = rows.astype(BF16)

    plane_start(1, answer, returned, small)
    value_pick = [
        pick_rows(value_expert[k], value_place[k], small, 0, experts * small).astype(BF16) for k in range(2)
    ]
    output_pick = [
        pick_rows(output_expert[k], output_place[k], small, capacity, experts * small).astype(BF16)
        for k in range(2)
    ]
    plane_wait(1, answer, returned, small)
    got = attention_step(
        queries[...],
        key_vectors[...],
        gate_logits[...],
        returned[...],
        value_hot,
        output_hot,
        value_pick,
        output_pick,
    )
    gated[...] = got[3]
    plane_start(2, gated, held_rows, small)
    query_grad[...] = got[0]
    key_grad[...] = got[1]
    logit_grad[...] = got[2]
    out_ids = lax.broadcasted_iota(jnp.int32, (block, small), 0)
    in_ids = lax.broadcasted_iota(jnp.int32, (block, small), 1)
    twice = out_ids - jnp.where(out_ids >= 2 * capacity, 2 * capacity, 0)
    fourfold = twice - jnp.where(twice >= capacity, capacity, 0)
    repeat_two = jnp.where(in_ids == twice, 1.0, 0.0).astype(BF16)
    repeat_four = jnp.where(in_ids == fourfold, 1.0, 0.0).astype(BF16)
    place_ids = lax.broadcasted_iota(jnp.int32, (block, head_size), 0)
    in_quarter = [
        (place_ids >= q * capacity) & (place_ids < (q + 1) * capacity) for q in range(4)
    ]
    plane_wait(2, gated, held_rows, small)
    for e in range(experts):
        rows = held_rows[e * small : (e + 1) * small, :]
        for repeat, target in ((repeat_two, wide), (repeat_four, spread)):
            copies = contract(repeat, rows, ((1,), (0,)))
            target[e * block : (e + 1) * block, :] = jnp.concatenate(
                [jnp.where(mask, copies, 0.0) for mask in in_quarter], axis=1
            ).astype(BF16)

    for c in range(half // tile):
        grads = contract(held[:, c * tile : (c + 1) * tile], wide[...], ((0,), (0,))).astype(BF16)
        for h in range(2):
            for s in range(tile // shard_rows):
                row = (h * half + c * tile) // shard_rows + s
                parts[row % 2, row // 2] = grads[
                    s * shard_rows : (s + 1) * shard_rows, h * 2 * head_size : (h + 1) * 2 * head_size
                ]
    pair_copy.start()
    for c in range(experts // chunk):
        span = slice(c * chunk * block, (c + 1) * chunk * block)
        back[span, :] = contract(spread[span, :], quarter_bank[...], ((1,), (1,))).astype(BF16)
    pair_copy.wait_recv()
    for k in range(chips):
        staged[k] = (parts[core, k].astype(F32) + pair[k].astype(F32)).astype(BF16)

    @pl.loop(1, chips)
    def _(j):
        sum_copy(j).start()

    plane_start(3, back, back_in, block)
    token_pick = [pick_sum(value_expert, value_place, block, q * capacity, width) for q in range(4)]
    plane_wait(3, back, back_in, block)
    for q in range(4):
        token_grad[:, q * quarter : (q + 1) * quarter] = contract(
            token_pick[q], back_in[...], ((1,), (0,))
        ).astype(BF16)

    landed[z] = staged[z]

    @pl.loop(1, chips)
    def _(j):
        sum_copy(j).wait_recv()

    total = landed[0].astype(F32)
    for k in range(1, chips):
        total = total + landed[k].astype(F32)
    total = total / groups
    value_weight_grad[...] = total[:, :head_size]
    output_weight_grad[...] = total[:, head_size:]

    plane_drain(0, sent, held, block)
    plane_drain(1, answer, returned, small)
    plane_drain(2, gated, held_rows, small)
    plane_drain(3, back, back_in, block)
    pair_copy.wait_send()

    @pl.loop(1, chips)
    def _(j):
        shard_copy(j).wait_send()
        sum_copy(j).wait_send()

    @pl.loop(0, chips)
    def _(j):
        forward_of(j).wait_send()


def on_device(
    tokens,
    queries,
    key_vectors,
    gate_logits,
    value_routes,
    output_routes,
    value_weight,
    output_weight,
    cotangent,
):
    tok_rows, features = tokens.shape
    head_size = queries.shape[1]
    experts = gate_logits.shape[1] // 2
    capacity = 5 * tok_rows // (2 * experts)
    groups = lax.axis_size("dp")
    chips = groups // 2
    shard_rows = features // groups
    small = 48
    block = 4 * capacity
    shard = jnp.concatenate([value_weight[0], output_weight[0]], axis=1)
    vmem = pl.BlockSpec(memory_space=pltpu.VMEM)

    def room(*shape):
        return pltpu.VMEM(shape, BF16)

    outs = pl.pallas_call(
        functools.partial(kernel, groups),
        out_shape=(
            jax.ShapeDtypeStruct((tok_rows, features), BF16),
            jax.ShapeDtypeStruct((tok_rows, head_size), BF16),
            jax.ShapeDtypeStruct((tok_rows, head_size), BF16),
            jax.ShapeDtypeStruct((tok_rows, 2 * experts), F32),
            jax.ShapeDtypeStruct((shard_rows, head_size), F32),
            jax.ShapeDtypeStruct((shard_rows, head_size), F32),
        ),
        in_specs=[vmem] * 8,
        out_specs=(vmem,) * 6,
        scratch_shapes=[
            room(experts * block, features // 2),
            room(experts * block, features // 2),
            room(features, 2 * head_size),
            room(features // 4, 4 * head_size),
            room(experts * small, head_size),
            room(experts * small, head_size),
            room(experts * small, head_size),
            room(experts * small, head_size),
            room(experts * block, 4 * head_size),
            room(experts * block, 4 * head_size),
            room(2, chips, shard_rows, 2 * head_size),
            room(chips, shard_rows, 2 * head_size),
            room(chips, shard_rows, 2 * head_size),
            room(chips, shard_rows, 2 * head_size),
            room(experts * block, features // 4),
            room(experts * block, features // 4),
            pltpu.SemaphoreType.DMA((4, experts)),
            pltpu.SemaphoreType.DMA((4, experts)),
            pltpu.SemaphoreType.DMA((2, chips)),
            pltpu.SemaphoreType.DMA((2, chips)),
            pltpu.SemaphoreType.DMA((chips,)),
            pltpu.SemaphoreType.DMA((chips,)),
            pltpu.SemaphoreType.DMA,
            pltpu.SemaphoreType.DMA,
            pltpu.SemaphoreType.DMA((5,)),
        ],
        compiler_params=pltpu.CompilerParams(collective_id=0, has_side_effects=True),
    )(tokens, queries, key_vectors, gate_logits, value_routes, output_routes, shard, cotangent)
    return outs[:4] + (outs[4][None], outs[5][None])


def solution(mesh):
    rows = P(("dp", "expert"), None)
    bank = P("expert", "dp", None)
    return jax.shard_map(
        on_device,
        mesh=mesh,
        in_specs=(rows,) * 6 + (bank, bank, rows),
        out_specs=(rows,) * 4 + (bank, bank),
        check_vma=False,
    )
```

```python
import functools
import math

import jax
import jax.numpy as jnp
from jax import lax
from jax.experimental import pallas as pl
from jax.experimental.pallas import tpu as pltpu
from jax.sharding import PartitionSpec as P

BF16 = jnp.bfloat16
F32 = jnp.float32
MESH = pl.DeviceIdType.MESH
SIDE = 4
RELAYED = (
    ((1, 2), (0, 3), (1, 3)),
    ((3, 2), (0, 3), (3, 3)),
    ((2, 1), (3, 1), (3, 0)),
    ((2, 3), (3, 3), (3, 0)),
)


def contract(left, right, dims):
    return lax.dot_general(left, right, (dims, ((), ())), preferred_element_type=F32)


def route_ranks(routes, experts):
    tokens = routes.shape[1]
    expert_ids = lax.broadcasted_iota(jnp.int32, (experts, tokens), 0)
    hots = [jnp.where(expert_ids == routes[k : k + 1, :], 1.0, 0.0).astype(F32) for k in range(2)]
    row_ids = lax.broadcasted_iota(jnp.int32, (tokens, tokens), 0)
    col_ids = lax.broadcasted_iota(jnp.int32, (tokens, tokens), 1)
    earlier = jnp.where(row_ids < col_ids, 1.0, 0.0).astype(BF16)
    rank = contract((hots[0] + hots[1]).astype(BF16), earlier, ((1,), (0,)))
    places = [jnp.sum(hot * rank, axis=0, keepdims=True) for hot in hots]
    return [routes[k : k + 1, :].astype(F32) for k in range(2)] + places


def pick_rows(expert, place, stride, offset, width):
    slot_ids = lax.broadcasted_iota(jnp.int32, (expert.shape[0], width), 1)
    return jnp.where(slot_ids == expert * stride + place + offset, 1.0, 0.0).astype(F32)


def chosen_rows(expert, place, stride, offset, width):
    slot_ids = lax.broadcasted_iota(jnp.int32, (width, expert[0].shape[1]), 0)
    slots = [(expert[k] * stride + place[k] + offset).astype(jnp.int32) for k in range(2)]
    return jnp.where((slot_ids == slots[0]) | (slot_ids == slots[1]), 1.0, 0.0).astype(BF16)


def attention_step(queries, keys, gate_logits, returned, value_hot, output_hot, value_pick, output_pick):
    rows, head_size = queries.shape
    experts = gate_logits.shape[1] // 2
    gates = jax.nn.sigmoid(gate_logits)
    value_gate = [jnp.sum(hot * gates[:, :experts], axis=1, keepdims=True) for hot in value_hot]
    output_gate = [jnp.sum(hot * gates[:, experts:], axis=1, keepdims=True) for hot in output_hot]
    expert_value = [contract(pick, returned, ((1,), (0,))) for pick in value_pick]
    head_back = [contract(pick, returned, ((1,), (0,))) for pick in output_pick]
    mixed_value = (value_gate[0] * expert_value[0] + value_gate[1] * expert_value[1]).astype(BF16)
    scores = contract(queries, keys, ((1,), (1,))) / math.sqrt(head_size)
    row_ids = lax.broadcasted_iota(jnp.int32, (rows, rows), 0)
    col_ids = lax.broadcasted_iota(jnp.int32, (rows, rows), 1)
    scores = jnp.where(row_ids >= col_ids, scores, -1e30)
    exponent = jnp.exp(scores - jnp.max(scores, axis=1, keepdims=True))
    probs = exponent / jnp.sum(exponent, axis=1, keepdims=True)
    weights = probs.astype(BF16)
    hidden = contract(weights, mixed_value, ((1,), (0,))).astype(BF16)
    hidden_wide = hidden.astype(F32)
    hidden_grad = (output_gate[0] * head_back[0] + output_gate[1] * head_back[1]).astype(BF16)
    prob_grad = contract(hidden_grad, mixed_value, ((1,), (1,)))
    score_grad = probs * (prob_grad - jnp.sum(prob_grad * probs, axis=1, keepdims=True))
    scaled_grad = (score_grad / math.sqrt(head_size)).astype(BF16)
    query_grad = contract(scaled_grad, keys, ((1,), (0,))).astype(BF16)
    key_grad = contract(scaled_grad, queries, ((0,), (0,))).astype(BF16)
    value_grad = contract(weights, hidden_grad, ((0,), (0,))).astype(BF16)
    value_wide = value_grad.astype(F32)
    gated_value = [(gate * value_wide).astype(BF16) for gate in value_gate]
    gated_hidden = [(gate * hidden_wide).astype(BF16) for gate in output_gate]
    logit_value = 0.0
    logit_output = 0.0
    for k in range(2):
        slope = jnp.sum(value_wide * expert_value[k], axis=1, keepdims=True)
        logit_value += value_hot[k] * (slope * value_gate[k] * (1.0 - value_gate[k]))
        slope = jnp.sum(hidden_wide * head_back[k], axis=1, keepdims=True)
        logit_output += output_hot[k] * (slope * output_gate[k] * (1.0 - output_gate[k]))
    logit_grad = jnp.concatenate([logit_value, logit_output], axis=1)
    sent_rows = contract(
        jnp.concatenate(value_pick + output_pick, axis=0),
        jnp.concatenate(gated_value + gated_hidden, axis=0),
        ((0,), (0,)),
    ).astype(BF16)
    return query_grad, key_grad, logit_grad, sent_rows


def kernel(
    groups,
    tokens,
    queries,
    key_vectors,
    gate_logits,
    value_routes,
    output_routes,
    value_weight,
    output_weight,
    cotangent,
    token_grad,
    query_grad,
    key_grad,
    logit_grad,
    value_weight_grad,
    output_weight_grad,
    shard,
    sent,
    held,
    relay,
    back_relay,
    banks,
    quarter_bank,
    answer,
    returned,
    gated,
    held_rows,
    wide,
    spread,
    parts,
    pair,
    staged,
    landed,
    back,
    back_in,
    send_x,
    recv_x,
    send_z,
    recv_z,
    send_f,
    recv_f,
    send_p,
    recv_p,
    send_r,
    recv_r,
    local,
):
    tok_rows, features = tokens.shape
    head_size = queries.shape[1]
    experts = gate_logits.shape[0] // 2
    capacity = 5 * tok_rows // (2 * experts)
    half, quarter = features // 2, features // 4
    chips = groups // 2
    shard_rows = features // groups
    block = 4 * capacity
    small = answer.shape[0] // experts
    me_dp = lax.axis_index("dp")
    me_ex = lax.axis_index("expert")
    z, core = me_dp // 2, me_dp % 2
    y, x = me_ex // SIDE, me_ex % SIDE
    partner = z * 2 + 1 - core

    def plane_peer(i):
        return ((y + i // SIDE) % SIDE) * SIDE + (x + i % SIDE) % SIDE

    def chip_step(j):
        return (j % 2) * ((j + 1) // 2) + (1 - j % 2) * (chips - j // 2)

    def chip_peer(j):
        return ((z + chip_step(j)) % chips) * 2 + core

    def chip_source(j):
        return ((z + chips - chip_step(j)) % chips) * 2 + core

    def window(ref, index, size):
        return ref.at[pl.ds(pl.multiple_of(index * size, 16), size)]

    def plane_copy(phase, source, target, size, i):
        peer = plane_peer(i)
        return pltpu.make_async_remote_copy(
            src_ref=window(source, peer, size),
            dst_ref=window(target, me_ex, size),
            send_sem=send_x.at[phase, i],
            recv_sem=recv_x.at[phase, i],
            device_id={"expert": peer},
            device_id_type=MESH,
        )

    def plane_own(phase, source, target, size):
        return pltpu.make_async_copy(
            window(source, me_ex, size), window(target, me_ex, size), local.at[phase]
        )

    def plane_start(phase, source, target, size):
        @pl.loop(1, experts)
        def _(i):
            plane_copy(phase, source, target, size, i).start()

        plane_own(phase, source, target, size).start()

    def plane_wait(phase, source, target, size):
        plane_own(phase, source, target, size).wait()

        @pl.loop(1, experts)
        def _(i):
            plane_copy(phase, source, target, size, i).wait_recv()

    def step(dy, dx):
        return ((y + dy) % SIDE) * SIDE + (x + dx) % SIDE

    def first_leg(phase, source, buffer, size, r):
        (dy, dx), via, _ = RELAYED[r]
        return pltpu.make_async_remote_copy(
            src_ref=window(source, step(dy, dx), size),
            dst_ref=buffer.at[r],
            send_sem=send_x.at[phase, dy * SIDE + dx],
            recv_sem=recv_r.at[phase // 3, r],
            device_id={"expert": step(*via)},
            device_id_type=MESH,
        )

    def last_leg(phase, buffer, target, size, r):
        (dy, dx), via, leg = RELAYED[r]
        return pltpu.make_async_remote_copy(
            src_ref=buffer.at[r],
            dst_ref=window(target, step(SIDE - via[0], SIDE - via[1]), size),
            send_sem=send_r.at[phase // 3, r],
            recv_sem=recv_x.at[phase, dy * SIDE + dx],
            device_id={"expert": step(*leg)},
            device_id_type=MESH,
        )

    direct = [i for i in range(1, SIDE * SIDE) if (i // SIDE, i % SIDE) not in [r[0] for r in RELAYED]]

    def balanced_start(phase, source, buffer, target, size):
        for r in range(len(RELAYED)):
            first_leg(phase, source, buffer, size, r).start()
        for i in sorted(direct, key=lambda i: -(i // SIDE == 2) - (i % SIDE == 2)):
            plane_copy(phase, source, target, size, i).start()
        plane_own(phase, source, target, size).start()

    def balanced_relay(phase, source, buffer, target, size):
        for r in range(len(RELAYED)):
            first_leg(phase, source, buffer, size, r).wait_recv()
            last_leg(phase, buffer, target, size, r).start()

    def balanced_drain(phase, source, buffer, target, size):
        plane_drain(phase, source, target, size)
        for r in range(len(RELAYED)):
            last_leg(phase, buffer, target, size, r).wait_send()

    def plane_drain(phase, source, target, size):
        @pl.loop(1, experts)
        def _(i):
            plane_copy(phase, source, target, size, i).wait_send()

    def shard_copy(j):
        return pltpu.make_async_remote_copy(
            src_ref=shard,
            dst_ref=window(banks, me_dp, shard_rows),
            send_sem=send_z.at[0, j],
            recv_sem=recv_z.at[0, j],
            device_id={"dp": chip_peer(j)},
            device_id_type=MESH,
        )

    def forward_copy(j, source, row):
        return pltpu.make_async_remote_copy(
            src_ref=source,
            dst_ref=window(banks, row, shard_rows),
            send_sem=send_f.at[j],
            recv_sem=recv_f.at[j],
            device_id={"dp": partner},
            device_id_type=MESH,
        )

    def forward_of(j):
        row = chip_source(j)
        return forward_copy(j, window(banks, row, shard_rows), row)

    def sum_copy(j):
        return pltpu.make_async_remote_copy(
            src_ref=staged.at[(z + chip_step(j)) % chips],
            dst_ref=landed.at[z],
            send_sem=send_z.at[1, j],
            recv_sem=recv_z.at[1, j],
            device_id={"dp": chip_peer(j)},
            device_id_type=MESH,
        )

    pair_copy = pltpu.make_async_remote_copy(
        src_ref=parts.at[1 - core],
        dst_ref=pair,
        send_sem=send_p,
        recv_sem=recv_p,
        device_id={"dp": partner},
        device_id_type=MESH,
    )

    barrier = pltpu.get_barrier_semaphore()

    @pl.loop(1, experts)
    def _(i):
        pl.semaphore_signal(barrier, inc=1, device_id={"expert": plane_peer(i)}, device_id_type=MESH)

    @pl.loop(1, chips)
    def _(j):
        pl.semaphore_signal(barrier, inc=1, device_id={"dp": chip_peer(j)}, device_id_type=MESH)

    pl.semaphore_signal(barrier, inc=1, device_id={"dp": partner}, device_id_type=MESH)

    shard[:, :head_size] = value_weight[0]
    shard[:, head_size:] = output_weight[0]
    own_shard = pltpu.make_async_copy(shard, window(banks, me_dp, shard_rows), local.at[4])
    own_shard.start()
    value_stats = route_ranks(value_routes[...], experts)
    output_stats = route_ranks(output_routes[...], experts)
    width = experts * block
    chosen = jnp.concatenate(
        [
            chosen_rows(stats[:2], stats[2:], block, offset, width)
            for stats, offset in (
                (value_stats, 0),
                (output_stats, capacity),
                (value_stats, 2 * capacity),
                (output_stats, 3 * capacity),
            )
        ],
        axis=1,
    )
    tile = 256
    cut = width // 2
    for c in range(half // tile):
        low = pl.ds(c * tile, tile)
        high = pl.ds(half + c * tile, tile)
        rows = jnp.concatenate([tokens[:, low], cotangent[:, low], tokens[:, high], cotangent[:, high]], axis=0)
        for part in range(2):
            sent[part * cut : (part + 1) * cut, low] = contract(
                chosen[part * cut : (part + 1) * cut, :], rows, ((1,), (0,))
            ).astype(BF16)

    pl.semaphore_wait(barrier, experts - 1 + chips)
    balanced_start(0, sent, relay, held, block)

    @pl.loop(1, chips)
    def _(j):
        shard_copy(j).start()

    forward_copy(0, shard, me_dp).start()
    columns = jnp.concatenate(value_stats + output_stats, axis=0).T.astype(jnp.int32)
    value_expert, value_place, output_expert, output_place = [
        [columns[:, 2 * n + k : 2 * n + k + 1] for k in range(2)] for n in range(4)
    ]
    expert_ids = lax.broadcasted_iota(jnp.int32, (tok_rows, experts), 1)
    value_hot, output_hot = [
        [jnp.where(expert_ids == column, 1.0, 0.0).astype(F32) for column in pair_of]
        for pair_of in (value_expert, output_expert)
    ]

    def pick_sum(expert, place, stride, offset, width):
        picks = [pick_rows(expert[k], place[k], stride, offset, width) for k in range(2)]
        return (picks[0] + picks[1]).astype(BF16)

    balanced_relay(0, sent, relay, held, block)

    @pl.loop(1, chips)
    def _(j):
        shard_copy(j).wait_recv()
        forward_of(j).start()

    own_shard.wait()

    @pl.loop(0, chips)
    def _(j):
        forward_of(j).wait_recv()

    bank_pair = jnp.concatenate([banks[:half, :], banks[half:, :]], axis=1)
    for q in range(4):
        quarter_bank[:, q * head_size : (q + 1) * head_size] = banks[q * quarter : (q + 1) * quarter, :head_size]

    plane_wait(0, sent, held, block)

    row_ids = lax.broadcasted_iota(jnp.int32, (2 * capacity, head_size), 0)
    chunk = 4
    for c in range(experts // chunk):
        both = contract(held[c * chunk * block : (c + 1) * chunk * block, :], bank_pair, ((1,), (0,)))
        for k in range(chunk):
            top = both[k * block : k * block + 2 * capacity, : 2 * head_size]
            low = both[k * block + 2 * capacity : (k + 1) * block, 2 * head_size :]
            total = top + low
            rows = jnp.where(row_ids < capacity, total[:, :head_size], total[:, head_size:])
            rows = jnp.concatenate([rows, jnp.zeros((small - 2 * capacity, head_size), F32)], axis=0)
            e = c * chunk + k
            answer[e * small : (e + 1) * small, :] = rows.astype(BF16)

    plane_start(1, answer, returned, small)
    value_pick = [
        pick_rows(value_expert[k], value_place[k], small, 0, experts * small).astype(BF16) for k in range(2)
    ]
    output_pick = [
        pick_rows(output_expert[k], output_place[k], small, capacity, experts * small).astype(BF16)
        for k in range(2)
    ]
    plane_wait(1, answer, returned, small)
    got = attention_step(
        queries[...],
        key_vectors[...],
        gate_logits[...].T,
        returned[...],
        value_hot,
        output_hot,
        value_pick,
        output_pick,
    )
    gated[...] = got[3]
    plane_start(2, gated, held_rows, small)
    query_grad[...] = got[0]
    key_grad[...] = got[1]
    logit_grad[...] = got[2].T
    out_ids = lax.broadcasted_iota(jnp.int32, (block, small), 0)
    in_ids = lax.broadcasted_iota(jnp.int32, (block, small), 1)
    twice = out_ids - jnp.where(out_ids >= 2 * capacity, 2 * capacity, 0)
    fourfold = twice - jnp.where(twice >= capacity, capacity, 0)
    repeat_two = jnp.where(in_ids == twice, 1.0, 0.0).astype(BF16)
    repeat_four = jnp.where(in_ids == fourfold, 1.0, 0.0).astype(BF16)
    place_ids = lax.broadcasted_iota(jnp.int32, (block, head_size), 0)
    in_quarter = [
        (place_ids >= q * capacity) & (place_ids < (q + 1) * capacity) for q in range(4)
    ]
    plane_wait(2, gated, held_rows, small)
    for e in range(experts):
        rows = held_rows[e * small : (e + 1) * small, :]
        for repeat, target in ((repeat_two, wide), (repeat_four, spread)):
            copies = contract(repeat, rows, ((1,), (0,)))
            target[e * block : (e + 1) * block, :] = jnp.concatenate(
                [jnp.where(mask, copies, 0.0) for mask in in_quarter], axis=1
            ).astype(BF16)

    for c in range(half // tile):
        grads = contract(held[:, c * tile : (c + 1) * tile], wide[...], ((0,), (0,))).astype(BF16)
        for h in range(2):
            for s in range(tile // shard_rows):
                row = (h * half + c * tile) // shard_rows + s
                parts[row % 2, row // 2] = grads[
                    s * shard_rows : (s + 1) * shard_rows, h * 2 * head_size : (h + 1) * 2 * head_size
                ]
    pair_copy.start()
    for c in range(experts // chunk):
        span = slice(c * chunk * block, (c + 1) * chunk * block)
        back[span, :] = contract(spread[span, :], quarter_bank[...], ((1,), (1,))).astype(BF16)
    pair_copy.wait_recv()
    for k in range(chips):
        staged[k] = (parts[core, k].astype(F32) + pair[k].astype(F32)).astype(BF16)

    @pl.loop(1, chips)
    def _(j):
        sum_copy(j).start()

    balanced_start(3, back, back_relay, back_in, block)
    balanced_relay(3, back, back_relay, back_in, block)
    token_pick = [pick_sum(value_expert, value_place, block, q * capacity, width) for q in range(4)]
    plane_wait(3, back, back_in, block)
    for q in range(4):
        token_grad[:, q * quarter : (q + 1) * quarter] = contract(
            token_pick[q], back_in[...], ((1,), (0,))
        ).astype(BF16)

    landed[z] = staged[z]

    @pl.loop(1, chips)
    def _(j):
        sum_copy(j).wait_recv()

    total = landed[0].astype(F32)
    for k in range(1, chips):
        total = total + landed[k].astype(F32)
    total = total / groups
    value_weight_grad[...] = total[:, :head_size]
    output_weight_grad[...] = total[:, head_size:]

    balanced_drain(0, sent, relay, held, block)
    plane_drain(1, answer, returned, small)
    plane_drain(2, gated, held_rows, small)
    balanced_drain(3, back, back_relay, back_in, block)
    pair_copy.wait_send()

    @pl.loop(1, chips)
    def _(j):
        shard_copy(j).wait_send()
        sum_copy(j).wait_send()

    @pl.loop(0, chips)
    def _(j):
        forward_of(j).wait_send()


def hand_over(*refs):
    for source, target in zip(refs[:6], refs[6:]):
        target[...] = source[...]


def on_device(
    tokens,
    queries,
    key_vectors,
    gate_logits,
    value_routes,
    output_routes,
    value_weight,
    output_weight,
    cotangent,
):
    tok_rows, features = tokens.shape
    head_size = queries.shape[1]
    experts = gate_logits.shape[1] // 2
    capacity = 5 * tok_rows // (2 * experts)
    groups = lax.axis_size("dp")
    chips = groups // 2
    shard_rows = features // groups
    small = 48
    block = 4 * capacity
    vmem = pl.BlockSpec(memory_space=pltpu.VMEM)

    def room(*shape):
        return pltpu.VMEM(shape, BF16)

    outs = pl.pallas_call(
        functools.partial(kernel, groups),
        out_shape=(
            jax.ShapeDtypeStruct((tok_rows, features), BF16),
            jax.ShapeDtypeStruct((tok_rows, head_size), BF16),
            jax.ShapeDtypeStruct((tok_rows, head_size), BF16),
            jax.ShapeDtypeStruct((2 * experts, tok_rows), F32),
            jax.ShapeDtypeStruct((shard_rows, head_size), F32),
            jax.ShapeDtypeStruct((shard_rows, head_size), F32),
        ),
        in_specs=[vmem] * 9,
        out_specs=(vmem,) * 6,
        scratch_shapes=[
            room(shard_rows, 2 * head_size),
            room(experts * block, features // 2),
            room(experts * block, features // 2),
            room(len(RELAYED), block, features // 2),
            room(len(RELAYED), block, features // 4),
            room(features, 2 * head_size),
            room(features // 4, 4 * head_size),
            room(experts * small, head_size),
            room(experts * small, head_size),
            room(experts * small, head_size),
            room(experts * small, head_size),
            room(experts * block, 4 * head_size),
            room(experts * block, 4 * head_size),
            room(2, chips, shard_rows, 2 * head_size),
            room(chips, shard_rows, 2 * head_size),
            room(chips, shard_rows, 2 * head_size),
            room(chips, shard_rows, 2 * head_size),
            room(experts * block, features // 4),
            room(experts * block, features // 4),
            pltpu.SemaphoreType.DMA((4, experts)),
            pltpu.SemaphoreType.DMA((4, experts)),
            pltpu.SemaphoreType.DMA((2, chips)),
            pltpu.SemaphoreType.DMA((2, chips)),
            pltpu.SemaphoreType.DMA((chips,)),
            pltpu.SemaphoreType.DMA((chips,)),
            pltpu.SemaphoreType.DMA,
            pltpu.SemaphoreType.DMA,
            pltpu.SemaphoreType.DMA((2, len(RELAYED))),
            pltpu.SemaphoreType.DMA((2, len(RELAYED))),
            pltpu.SemaphoreType.DMA((5,)),
        ],
        compiler_params=pltpu.CompilerParams(collective_id=0, has_side_effects=True),
    )(
        tokens,
        queries,
        key_vectors,
        gate_logits.T,
        value_routes.T,
        output_routes.T,
        value_weight,
        output_weight,
        cotangent,
    )
    outs = pl.pallas_call(
        hand_over,
        out_shape=tuple(jax.ShapeDtypeStruct(out.shape, out.dtype) for out in outs),
        in_specs=[vmem] * 6,
        out_specs=(vmem,) * 6,
    )(*outs)
    return outs[:3] + (outs[3].T, outs[4][None], outs[5][None])


def solution(mesh):
    rows = P(("dp", "expert"), None)
    bank = P("expert", "dp", None)
    return jax.shard_map(
        on_device,
        mesh=mesh,
        in_specs=(rows,) * 6 + (bank, bank, rows),
        out_specs=(rows,) * 4 + (bank, bank),
        check_vma=False,
    )
```

```python
import functools
import math

import jax
import jax.numpy as jnp
from jax import lax
from jax.experimental import pallas as pl
from jax.experimental.pallas import tpu as pltpu
from jax.sharding import PartitionSpec as P

BF16 = jnp.bfloat16
F32 = jnp.float32
MESH = pl.DeviceIdType.MESH
SIDE = 4
RELAYED = (
    ((1, 2), (0, 3), (1, 3)),
    ((3, 2), (0, 3), (3, 3)),
    ((2, 1), (3, 1), (3, 0)),
    ((2, 3), (3, 3), (3, 0)),
)


def contract(left, right, dims):
    return lax.dot_general(left, right, (dims, ((), ())), preferred_element_type=F32)


def route_ranks(routes, experts):
    tokens = routes.shape[1]
    expert_ids = lax.broadcasted_iota(jnp.int32, (experts, tokens), 0)
    hots = [jnp.where(expert_ids == routes[k : k + 1, :], 1.0, 0.0).astype(F32) for k in range(2)]
    row_ids = lax.broadcasted_iota(jnp.int32, (tokens, tokens), 0)
    col_ids = lax.broadcasted_iota(jnp.int32, (tokens, tokens), 1)
    earlier = jnp.where(row_ids < col_ids, 1.0, 0.0).astype(BF16)
    rank = contract((hots[0] + hots[1]).astype(BF16), earlier, ((1,), (0,)))
    places = [jnp.sum(hot * rank, axis=0, keepdims=True) for hot in hots]
    return [routes[k : k + 1, :].astype(F32) for k in range(2)] + places


def pick_rows(expert, place, stride, offset, width):
    slot_ids = lax.broadcasted_iota(jnp.int32, (expert.shape[0], width), 1)
    return jnp.where(slot_ids == expert * stride + place + offset, 1.0, 0.0).astype(F32)


def chosen_rows(expert, place, stride, offset, width):
    slot_ids = lax.broadcasted_iota(jnp.int32, (width, expert[0].shape[1]), 0)
    slots = [(expert[k] * stride + place[k] + offset).astype(jnp.int32) for k in range(2)]
    return jnp.where((slot_ids == slots[0]) | (slot_ids == slots[1]), 1.0, 0.0).astype(BF16)


def attention_step(queries, keys, gate_logits, returned, value_hot, output_hot, value_pick, output_pick):
    rows, head_size = queries.shape
    experts = gate_logits.shape[1] // 2
    gates = jax.nn.sigmoid(gate_logits)
    value_gate = [jnp.sum(hot * gates[:, :experts], axis=1, keepdims=True) for hot in value_hot]
    output_gate = [jnp.sum(hot * gates[:, experts:], axis=1, keepdims=True) for hot in output_hot]
    expert_value = [contract(pick, returned, ((1,), (0,))) for pick in value_pick]
    head_back = [contract(pick, returned, ((1,), (0,))) for pick in output_pick]
    mixed_value = (value_gate[0] * expert_value[0] + value_gate[1] * expert_value[1]).astype(BF16)
    scores = contract(queries, keys, ((1,), (1,))) / math.sqrt(head_size)
    row_ids = lax.broadcasted_iota(jnp.int32, (rows, rows), 0)
    col_ids = lax.broadcasted_iota(jnp.int32, (rows, rows), 1)
    scores = jnp.where(row_ids >= col_ids, scores, -1e30)
    exponent = jnp.exp(scores - jnp.max(scores, axis=1, keepdims=True))
    probs = exponent / jnp.sum(exponent, axis=1, keepdims=True)
    weights = probs.astype(BF16)
    hidden = contract(weights, mixed_value, ((1,), (0,))).astype(BF16)
    hidden_wide = hidden.astype(F32)
    hidden_grad = (output_gate[0] * head_back[0] + output_gate[1] * head_back[1]).astype(BF16)
    prob_grad = contract(hidden_grad, mixed_value, ((1,), (1,)))
    score_grad = probs * (prob_grad - jnp.sum(prob_grad * probs, axis=1, keepdims=True))
    scaled_grad = (score_grad / math.sqrt(head_size)).astype(BF16)
    query_grad = contract(scaled_grad, keys, ((1,), (0,))).astype(BF16)
    key_grad = contract(scaled_grad, queries, ((0,), (0,))).astype(BF16)
    value_grad = contract(weights, hidden_grad, ((0,), (0,))).astype(BF16)
    value_wide = value_grad.astype(F32)
    gated_value = [(gate * value_wide).astype(BF16) for gate in value_gate]
    gated_hidden = [(gate * hidden_wide).astype(BF16) for gate in output_gate]
    logit_value = 0.0
    logit_output = 0.0
    for k in range(2):
        slope = jnp.sum(value_wide * expert_value[k], axis=1, keepdims=True)
        logit_value += value_hot[k] * (slope * value_gate[k] * (1.0 - value_gate[k]))
        slope = jnp.sum(hidden_wide * head_back[k], axis=1, keepdims=True)
        logit_output += output_hot[k] * (slope * output_gate[k] * (1.0 - output_gate[k]))
    logit_grad = jnp.concatenate([logit_value, logit_output], axis=1)
    sent_rows = contract(
        jnp.concatenate(value_pick + output_pick, axis=0),
        jnp.concatenate(gated_value + gated_hidden, axis=0),
        ((0,), (0,)),
    ).astype(BF16)
    return query_grad, key_grad, logit_grad, sent_rows


def kernel(
    groups,
    tokens,
    queries,
    key_vectors,
    gate_logits,
    value_routes,
    output_routes,
    value_weight,
    output_weight,
    cotangent,
    token_grad,
    query_grad,
    key_grad,
    logit_grad,
    value_weight_grad,
    output_weight_grad,
    shard,
    chosen,
    sent,
    held,
    relay,
    back_relay,
    sum_relay,
    banks,
    quarter_bank,
    answer,
    returned,
    gated,
    held_rows,
    wide,
    spread,
    parts,
    pair,
    staged,
    landed,
    back,
    back_in,
    send_x,
    recv_x,
    send_z,
    recv_z,
    send_f,
    recv_f,
    send_p,
    recv_p,
    send_r,
    recv_r,
    send_q,
    recv_q,
    local,
):
    tok_rows, features = tokens.shape
    head_size = queries.shape[1]
    experts = gate_logits.shape[0] // 2
    capacity = 5 * tok_rows // (2 * experts)
    half, quarter = features // 2, features // 4
    chips = groups // 2
    shard_rows = features // groups
    block = 4 * capacity
    small = answer.shape[0] // experts
    me_dp = lax.axis_index("dp")
    me_ex = lax.axis_index("expert")
    z, core = me_dp // 2, me_dp % 2
    y, x = me_ex // SIDE, me_ex % SIDE
    partner = z * 2 + 1 - core

    def plane_peer(i):
        return ((y + i // SIDE) % SIDE) * SIDE + (x + i % SIDE) % SIDE

    def chip_step(j):
        return (j % 2) * ((j + 1) // 2) + (1 - j % 2) * (chips - j // 2)

    def chip_peer(j):
        return ((z + chip_step(j)) % chips) * 2 + core

    def chip_source(j):
        return ((z + chips - chip_step(j)) % chips) * 2 + core

    def window(ref, index, size):
        return ref.at[pl.ds(pl.multiple_of(index * size, 16), size)]

    def plane_copy(phase, source, target, size, i):
        peer = plane_peer(i)
        return pltpu.make_async_remote_copy(
            src_ref=window(source, peer, size),
            dst_ref=window(target, me_ex, size),
            send_sem=send_x.at[phase, i],
            recv_sem=recv_x.at[phase, i],
            device_id={"expert": peer},
            device_id_type=MESH,
        )

    def plane_own(phase, source, target, size):
        return pltpu.make_async_copy(
            window(source, me_ex, size), window(target, me_ex, size), local.at[phase]
        )

    def plane_start(phase, source, target, size):
        @pl.loop(1, experts)
        def _(i):
            plane_copy(phase, source, target, size, i).start()

        plane_own(phase, source, target, size).start()

    def plane_wait(phase, source, target, size):
        plane_own(phase, source, target, size).wait()

        @pl.loop(1, experts)
        def _(i):
            plane_copy(phase, source, target, size, i).wait_recv()

    def step(dy, dx):
        return ((y + dy) % SIDE) * SIDE + (x + dx) % SIDE

    def first_leg(phase, source, buffer, size, r):
        (dy, dx), via, _ = RELAYED[r]
        return pltpu.make_async_remote_copy(
            src_ref=window(source, step(dy, dx), size),
            dst_ref=buffer.at[r],
            send_sem=send_x.at[phase, dy * SIDE + dx],
            recv_sem=recv_r.at[phase // 3, r],
            device_id={"expert": step(*via)},
            device_id_type=MESH,
        )

    def last_leg(phase, buffer, target, size, r):
        (dy, dx), via, leg = RELAYED[r]
        return pltpu.make_async_remote_copy(
            src_ref=buffer.at[r],
            dst_ref=window(target, step(SIDE - via[0], SIDE - via[1]), size),
            send_sem=send_r.at[phase // 3, r],
            recv_sem=recv_x.at[phase, dy * SIDE + dx],
            device_id={"expert": step(*leg)},
            device_id_type=MESH,
        )

    direct = [i for i in range(1, SIDE * SIDE) if (i // SIDE, i % SIDE) not in [r[0] for r in RELAYED]]

    def balanced_start(phase, source, buffer, target, size):
        for r in range(len(RELAYED)):
            first_leg(phase, source, buffer, size, r).start()
        for i in sorted(direct, key=lambda i: -(i // SIDE == 2) - (i % SIDE == 2)):
            plane_copy(phase, source, target, size, i).start()
        plane_own(phase, source, target, size).start()

    def balanced_relay(phase, source, buffer, target, size):
        for r in range(len(RELAYED)):
            first_leg(phase, source, buffer, size, r).wait_recv()
            last_leg(phase, buffer, target, size, r).start()

    def balanced_drain(phase, source, buffer, target, size):
        plane_drain(phase, source, target, size)
        for r in range(len(RELAYED)):
            last_leg(phase, buffer, target, size, r).wait_send()

    def plane_drain(phase, source, target, size):
        @pl.loop(1, experts)
        def _(i):
            plane_copy(phase, source, target, size, i).wait_send()

    def shard_copy(j):
        return pltpu.make_async_remote_copy(
            src_ref=shard,
            dst_ref=window(banks, me_dp, shard_rows),
            send_sem=send_z.at[0, j],
            recv_sem=recv_z.at[0, j],
            device_id={"dp": chip_peer(j)},
            device_id_type=MESH,
        )

    def forward_copy(j, source, row):
        return pltpu.make_async_remote_copy(
            src_ref=source,
            dst_ref=window(banks, row, shard_rows),
            send_sem=send_f.at[j],
            recv_sem=recv_f.at[j],
            device_id={"dp": partner},
            device_id_type=MESH,
        )

    def forward_of(j):
        row = chip_source(j)
        return forward_copy(j, window(banks, row, shard_rows), row)

    def sum_copy(j):
        return pltpu.make_async_remote_copy(
            src_ref=staged.at[(z + chip_step(j)) % chips],
            dst_ref=landed.at[z],
            send_sem=send_z.at[1, j],
            recv_sem=recv_z.at[1, j],
            device_id={"dp": chip_peer(j)},
            device_id_type=MESH,
        )

    pair_copy = pltpu.make_async_remote_copy(
        src_ref=parts.at[1 - core],
        dst_ref=pair,
        send_sem=send_p,
        recv_sem=recv_p,
        device_id={"dp": partner},
        device_id_type=MESH,
    )

    barrier = pltpu.get_barrier_semaphore()

    @pl.loop(1, experts)
    def _(i):
        pl.semaphore_signal(barrier, inc=1, device_id={"expert": plane_peer(i)}, device_id_type=MESH)

    @pl.loop(1, chips)
    def _(j):
        pl.semaphore_signal(barrier, inc=1, device_id={"dp": chip_peer(j)}, device_id_type=MESH)

    pl.semaphore_signal(barrier, inc=1, device_id={"dp": partner}, device_id_type=MESH)

    shard[:, :head_size] = value_weight[0]
    shard[:, head_size:] = output_weight[0]
    own_shard = pltpu.make_async_copy(shard, window(banks, me_dp, shard_rows), local.at[4])
    own_shard.start()
    value_stats = route_ranks(value_routes[...], experts)
    output_stats = route_ranks(output_routes[...], experts)
    width = experts * block
    chosen[...] = jnp.concatenate(
        [
            chosen_rows(stats[:2], stats[2:], block, offset, width)
            for stats, offset in (
                (value_stats, 0),
                (output_stats, capacity),
                (value_stats, 2 * capacity),
                (output_stats, 3 * capacity),
            )
        ],
        axis=1,
    )
    pl.semaphore_wait(barrier, experts - 1 + chips)
    reach = chips // 4
    for j in range(1, 2 * reach + 1):
        shard_copy(j).start()
    forward_copy(0, shard, me_dp).start()
    tile = 256
    stripe = SIDE * block

    def stripe_of(index):
        return pl.ds(pl.multiple_of(index * stripe, 16), stripe)

    plane_order = (2, 1, 3, 0)
    for dy in plane_order:
        target_rows = stripe_of((y + dy) % SIDE)
        for c in range(half // tile):
            low = pl.ds(c * tile, tile)
            high = pl.ds(half + c * tile, tile)
            rows = jnp.concatenate(
                [tokens[:, low], cotangent[:, low], tokens[:, high], cotangent[:, high]], axis=0
            )
            sent[target_rows, low] = contract(chosen[target_rows, :], rows, ((1,), (0,))).astype(BF16)
        for r in range(len(RELAYED)):
            if RELAYED[r][0][0] == dy:
                first_leg(0, sent, relay, block, r).start()
        for i in direct:
            if i // SIDE == dy:
                plane_copy(0, sent, held, block, i).start()
    plane_own(0, sent, held, block).start()
    columns = jnp.concatenate(value_stats + output_stats, axis=0).T.astype(jnp.int32)
    value_expert, value_place, output_expert, output_place = [
        [columns[:, 2 * n + k : 2 * n + k + 1] for k in range(2)] for n in range(4)
    ]
    expert_ids = lax.broadcasted_iota(jnp.int32, (tok_rows, experts), 1)
    value_hot, output_hot = [
        [jnp.where(expert_ids == column, 1.0, 0.0).astype(F32) for column in pair_of]
        for pair_of in (value_expert, output_expert)
    ]

    def pick_sum(expert, place, stride, offset, width):
        picks = [pick_rows(expert[k], place[k], stride, offset, width) for k in range(2)]
        return (picks[0] + picks[1]).astype(BF16)


    def onward(j, via):
        row = chip_source(via)
        return pltpu.make_async_remote_copy(
            src_ref=window(banks, row, shard_rows),
            dst_ref=window(banks, row, shard_rows),
            send_sem=send_z.at[0, j],
            recv_sem=recv_z.at[0, j],
            device_id={"dp": ((z + chip_step(j) + chips - chip_step(via)) % chips) * 2 + core},
            device_id_type=MESH,
        )

    for via in (2 * reach - 1, 2 * reach):
        shard_copy(via).wait_recv()
        for j in range(2 * reach + 1, chips):
            if j % 2 == via % 2:
                onward(j, via).start()
        forward_of(via).start()

    @pl.loop(1, 2 * reach - 1)
    def _(j):
        shard_copy(j).wait_recv()
        forward_of(j).start()

    balanced_relay(0, sent, relay, held, block)

    @pl.loop(2 * reach + 1, chips)
    def _(j):
        shard_copy(j).wait_recv()
        forward_of(j).start()

    own_shard.wait()

    @pl.loop(0, chips)
    def _(j):
        forward_of(j).wait_recv()

    bank_pair = jnp.concatenate([banks[:half, :], banks[half:, :]], axis=1)
    for q in range(4):
        quarter_bank[:, q * head_size : (q + 1) * head_size] = banks[q * quarter : (q + 1) * quarter, :head_size]

    row_ids = lax.broadcasted_iota(jnp.int32, (2 * capacity, head_size), 0)
    chunk = SIDE
    for dy in plane_order:
        source_y = (y + SIDE - dy) % SIDE
        for dx in range(SIDE):
            if dy or dx:
                plane_copy(0, sent, held, block, dy * SIDE + dx).wait_recv()
            else:
                plane_own(0, sent, held, block).wait()
        both = contract(held[stripe_of(source_y), :], bank_pair, ((1,), (0,)))
        blocks = []
        for k in range(chunk):
            top = both[k * block : k * block + 2 * capacity, : 2 * head_size]
            low = both[k * block + 2 * capacity : (k + 1) * block, 2 * head_size :]
            total = top + low
            rows = jnp.where(row_ids < capacity, total[:, :head_size], total[:, head_size:])
            blocks += [rows, jnp.zeros((small - 2 * capacity, head_size), F32)]
        spot = pl.ds(pl.multiple_of(source_y * SIDE * small, 16), SIDE * small)
        answer[spot, :] = jnp.concatenate(blocks, axis=0).astype(BF16)
        for dx in range(SIDE):
            i = ((SIDE - dy) % SIDE) * SIDE + dx
            if i:
                plane_copy(1, answer, returned, small, i).start()
            else:
                plane_own(1, answer, returned, small).start()

    value_pick = [
        pick_rows(value_expert[k], value_place[k], small, 0, experts * small).astype(BF16) for k in range(2)
    ]
    output_pick = [
        pick_rows(output_expert[k], output_place[k], small, capacity, experts * small).astype(BF16)
        for k in range(2)
    ]
    plane_wait(1, answer, returned, small)
    got = attention_step(
        queries[...],
        key_vectors[...],
        gate_logits[...].T,
        returned[...],
        value_hot,
        output_hot,
        value_pick,
        output_pick,
    )
    gated[...] = got[3]
    plane_start(2, gated, held_rows, small)
    query_grad[...] = got[0]
    key_grad[...] = got[1]
    logit_grad[...] = got[2].T
    out_ids = lax.broadcasted_iota(jnp.int32, (block, small), 0)
    in_ids = lax.broadcasted_iota(jnp.int32, (block, small), 1)
    twice = out_ids - jnp.where(out_ids >= 2 * capacity, 2 * capacity, 0)
    fourfold = twice - jnp.where(twice >= capacity, capacity, 0)
    repeat_two = jnp.where(in_ids == twice, 1.0, 0.0).astype(BF16)
    repeat_four = jnp.where(in_ids == fourfold, 1.0, 0.0).astype(BF16)
    place_ids = lax.broadcasted_iota(jnp.int32, (block, head_size), 0)
    in_quarter = [
        (place_ids >= q * capacity) & (place_ids < (q + 1) * capacity) for q in range(4)
    ]
    plane_wait(2, gated, held_rows, small)
    for e in range(experts):
        rows = held_rows[e * small : (e + 1) * small, :]
        for repeat, target in ((repeat_two, wide), (repeat_four, spread)):
            copies = contract(repeat, rows, ((1,), (0,)))
            target[e * block : (e + 1) * block, :] = jnp.concatenate(
                [jnp.where(mask, copies, 0.0) for mask in in_quarter], axis=1
            ).astype(BF16)

    for c in range(half // tile):
        grads = contract(held[:, c * tile : (c + 1) * tile], wide[...], ((0,), (0,))).astype(BF16)
        for h in range(2):
            for s in range(tile // shard_rows):
                row = (h * half + c * tile) // shard_rows + s
                parts[row % 2, row // 2] = grads[
                    s * shard_rows : (s + 1) * shard_rows, h * 2 * head_size : (h + 1) * 2 * head_size
                ]
    pair_copy.start()
    for c in range(experts // chunk):
        span = slice(c * chunk * block, (c + 1) * chunk * block)
        back[span, :] = contract(spread[span, :], quarter_bank[...], ((1,), (1,))).astype(BF16)
    pair_copy.wait_recv()
    for k in range(chips):
        staged[k] = (parts[core, k].astype(F32) + pair[k].astype(F32)).astype(BF16)

    @pl.loop(1, chips - 1)
    def _(j):
        sum_copy(j).start()

    quarter_turn = reach + core * (chips // 2)
    far_first = pltpu.make_async_remote_copy(
        src_ref=staged.at[(z + chips // 2) % chips],
        dst_ref=sum_relay,
        send_sem=send_z.at[1, chips - 1],
        recv_sem=recv_q,
        device_id={"dp": ((z + quarter_turn) % chips) * 2 + core},
        device_id_type=MESH,
    )
    far_last = pltpu.make_async_remote_copy(
        src_ref=sum_relay,
        dst_ref=landed.at[(z + chips - quarter_turn) % chips],
        send_sem=send_q,
        recv_sem=recv_z.at[1, chips - 1],
        device_id={"dp": ((z + quarter_turn) % chips) * 2 + core},
        device_id_type=MESH,
    )
    far_first.start()
    balanced_start(3, back, back_relay, back_in, block)
    balanced_relay(3, back, back_relay, back_in, block)
    far_first.wait_recv()
    far_last.start()
    token_pick = [pick_sum(value_expert, value_place, block, q * capacity, width) for q in range(4)]
    plane_wait(3, back, back_in, block)
    for q in range(4):
        token_grad[:, q * quarter : (q + 1) * quarter] = contract(
            token_pick[q], back_in[...], ((1,), (0,))
        ).astype(BF16)

    landed[z] = staged[z]

    @pl.loop(1, chips)
    def _(j):
        sum_copy(j).wait_recv()

    total = landed[0].astype(F32)
    for k in range(1, chips):
        total = total + landed[k].astype(F32)
    total = total / groups
    value_weight_grad[...] = total[:, :head_size]
    output_weight_grad[...] = total[:, head_size:]

    balanced_drain(0, sent, relay, held, block)
    plane_drain(1, answer, returned, small)
    plane_drain(2, gated, held_rows, small)
    balanced_drain(3, back, back_relay, back_in, block)
    pair_copy.wait_send()
    far_last.wait_send()

    @pl.loop(1, chips)
    def _(j):
        shard_copy(j).wait_send()
        sum_copy(j).wait_send()

    @pl.loop(0, chips)
    def _(j):
        forward_of(j).wait_send()


def hand_over(*refs):
    for source, target in zip(refs[:6], refs[6:]):
        target[...] = source[...]


def on_device(
    tokens,
    queries,
    key_vectors,
    gate_logits,
    value_routes,
    output_routes,
    value_weight,
    output_weight,
    cotangent,
):
    tok_rows, features = tokens.shape
    head_size = queries.shape[1]
    experts = gate_logits.shape[1] // 2
    capacity = 5 * tok_rows // (2 * experts)
    groups = lax.axis_size("dp")
    chips = groups // 2
    shard_rows = features // groups
    small = 48
    block = 4 * capacity
    vmem = pl.BlockSpec(memory_space=pltpu.VMEM)

    def room(*shape):
        return pltpu.VMEM(shape, BF16)

    outs = pl.pallas_call(
        functools.partial(kernel, groups),
        out_shape=(
            jax.ShapeDtypeStruct((tok_rows, features), BF16),
            jax.ShapeDtypeStruct((tok_rows, head_size), BF16),
            jax.ShapeDtypeStruct((tok_rows, head_size), BF16),
            jax.ShapeDtypeStruct((2 * experts, tok_rows), F32),
            jax.ShapeDtypeStruct((shard_rows, head_size), F32),
            jax.ShapeDtypeStruct((shard_rows, head_size), F32),
        ),
        in_specs=[vmem] * 9,
        out_specs=(vmem,) * 6,
        scratch_shapes=[
            room(shard_rows, 2 * head_size),
            room(experts * block, 4 * tok_rows),
            room(experts * block, features // 2),
            room(experts * block, features // 2),
            room(len(RELAYED), block, features // 2),
            room(len(RELAYED), block, features // 4),
            room(shard_rows, 2 * head_size),
            room(features, 2 * head_size),
            room(features // 4, 4 * head_size),
            room(experts * small, head_size),
            room(experts * small, head_size),
            room(experts * small, head_size),
            room(experts * small, head_size),
            room(experts * block, 4 * head_size),
            room(experts * block, 4 * head_size),
            room(2, chips, shard_rows, 2 * head_size),
            room(chips, shard_rows, 2 * head_size),
            room(chips, shard_rows, 2 * head_size),
            room(chips, shard_rows, 2 * head_size),
            room(experts * block, features // 4),
            room(experts * block, features // 4),
            pltpu.SemaphoreType.DMA((4, experts)),
            pltpu.SemaphoreType.DMA((4, experts)),
            pltpu.SemaphoreType.DMA((2, chips)),
            pltpu.SemaphoreType.DMA((2, chips)),
            pltpu.SemaphoreType.DMA((chips,)),
            pltpu.SemaphoreType.DMA((chips,)),
            pltpu.SemaphoreType.DMA,
            pltpu.SemaphoreType.DMA,
            pltpu.SemaphoreType.DMA((2, len(RELAYED))),
            pltpu.SemaphoreType.DMA((2, len(RELAYED))),
            pltpu.SemaphoreType.DMA,
            pltpu.SemaphoreType.DMA,
            pltpu.SemaphoreType.DMA((5,)),
        ],
        compiler_params=pltpu.CompilerParams(collective_id=0, has_side_effects=True),
    )(
        tokens,
        queries,
        key_vectors,
        gate_logits.T,
        value_routes.T,
        output_routes.T,
        value_weight,
        output_weight,
        cotangent,
    )
    outs = pl.pallas_call(
        hand_over,
        out_shape=tuple(jax.ShapeDtypeStruct(out.shape, out.dtype) for out in outs),
        in_specs=[vmem] * 6,
        out_specs=(vmem,) * 6,
    )(*outs)
    return outs[:3] + (outs[3].T, outs[4][None], outs[5][None])


def solution(mesh):
    rows = P(("dp", "expert"), None)
    bank = P("expert", "dp", None)
    return jax.shard_map(
        on_device,
        mesh=mesh,
        in_specs=(rows,) * 6 + (bank, bank, rows),
        out_specs=(rows,) * 4 + (bank, bank),
        check_vma=False,
    )
```

```python
import functools
import math

import jax
import jax.numpy as jnp
from jax import lax
from jax.experimental import pallas as pl
from jax.experimental.pallas import tpu as pltpu
from jax.sharding import PartitionSpec as P

BF16 = jnp.bfloat16
F32 = jnp.float32
MESH = pl.DeviceIdType.MESH
SIDE = 4
RELAYED = (
    ((1, 2), (0, 3), (1, 3)),
    ((3, 2), (0, 3), (3, 3)),
    ((2, 1), (3, 1), (3, 0)),
    ((2, 3), (3, 3), (3, 0)),
)


def contract(left, right, dims):
    return lax.dot_general(left, right, (dims, ((), ())), preferred_element_type=F32)


def route_ranks(routes, experts):
    tokens = routes.shape[1]
    expert_ids = lax.broadcasted_iota(jnp.int32, (experts, tokens), 0)
    hots = [jnp.where(expert_ids == routes[k : k + 1, :], 1.0, 0.0).astype(F32) for k in range(2)]
    row_ids = lax.broadcasted_iota(jnp.int32, (tokens, tokens), 0)
    col_ids = lax.broadcasted_iota(jnp.int32, (tokens, tokens), 1)
    earlier = jnp.where(row_ids < col_ids, 1.0, 0.0).astype(BF16)
    rank = contract((hots[0] + hots[1]).astype(BF16), earlier, ((1,), (0,)))
    places = [jnp.sum(hot * rank, axis=0, keepdims=True) for hot in hots]
    return [routes[k : k + 1, :].astype(F32) for k in range(2)] + places


def pick_rows(expert, place, stride, offset, width):
    slot_ids = lax.broadcasted_iota(jnp.int32, (expert.shape[0], width), 1)
    return jnp.where(slot_ids == expert * stride + place + offset, 1.0, 0.0).astype(F32)


def chosen_rows(expert, place, stride, offset, width):
    slot_ids = lax.broadcasted_iota(jnp.int32, (width, expert[0].shape[1]), 0)
    slots = [(expert[k] * stride + place[k] + offset).astype(jnp.int32) for k in range(2)]
    return jnp.where((slot_ids == slots[0]) | (slot_ids == slots[1]), 1.0, 0.0).astype(BF16)


def attention_step(queries, keys, gate_logits, returned, value_hot, output_hot, value_pick, output_pick):
    rows, head_size = queries.shape
    experts = gate_logits.shape[1] // 2
    gates = jax.nn.sigmoid(gate_logits)
    value_gate = [jnp.sum(hot * gates[:, :experts], axis=1, keepdims=True) for hot in value_hot]
    output_gate = [jnp.sum(hot * gates[:, experts:], axis=1, keepdims=True) for hot in output_hot]
    expert_value = [contract(pick, returned, ((1,), (0,))) for pick in value_pick]
    head_back = [contract(pick, returned, ((1,), (0,))) for pick in output_pick]
    mixed_value = (value_gate[0] * expert_value[0] + value_gate[1] * expert_value[1]).astype(BF16)
    scores = contract(queries, keys, ((1,), (1,))) / math.sqrt(head_size)
    row_ids = lax.broadcasted_iota(jnp.int32, (rows, rows), 0)
    col_ids = lax.broadcasted_iota(jnp.int32, (rows, rows), 1)
    scores = jnp.where(row_ids >= col_ids, scores, -1e30)
    exponent = jnp.exp(scores - jnp.max(scores, axis=1, keepdims=True))
    probs = exponent / jnp.sum(exponent, axis=1, keepdims=True)
    weights = probs.astype(BF16)
    hidden = contract(weights, mixed_value, ((1,), (0,))).astype(BF16)
    hidden_wide = hidden.astype(F32)
    hidden_grad = (output_gate[0] * head_back[0] + output_gate[1] * head_back[1]).astype(BF16)
    prob_grad = contract(hidden_grad, mixed_value, ((1,), (1,)))
    score_grad = probs * (prob_grad - jnp.sum(prob_grad * probs, axis=1, keepdims=True))
    scaled_grad = (score_grad / math.sqrt(head_size)).astype(BF16)
    query_grad = contract(scaled_grad, keys, ((1,), (0,))).astype(BF16)
    key_grad = contract(scaled_grad, queries, ((0,), (0,))).astype(BF16)
    value_grad = contract(weights, hidden_grad, ((0,), (0,))).astype(BF16)
    value_wide = value_grad.astype(F32)
    gated_value = [(gate * value_wide).astype(BF16) for gate in value_gate]
    gated_hidden = [(gate * hidden_wide).astype(BF16) for gate in output_gate]
    logit_value = 0.0
    logit_output = 0.0
    for k in range(2):
        slope = jnp.sum(value_wide * expert_value[k], axis=1, keepdims=True)
        logit_value += value_hot[k] * (slope * value_gate[k] * (1.0 - value_gate[k]))
        slope = jnp.sum(hidden_wide * head_back[k], axis=1, keepdims=True)
        logit_output += output_hot[k] * (slope * output_gate[k] * (1.0 - output_gate[k]))
    logit_grad = jnp.concatenate([logit_value, logit_output], axis=1)
    sent_rows = contract(
        jnp.concatenate(value_pick + output_pick, axis=0),
        jnp.concatenate(gated_value + gated_hidden, axis=0),
        ((0,), (0,)),
    ).astype(BF16)
    return query_grad, key_grad, logit_grad, sent_rows


def kernel(
    groups,
    tokens,
    queries,
    key_vectors,
    gate_logits,
    value_routes,
    output_routes,
    value_weight,
    output_weight,
    cotangent,
    token_grad,
    query_grad,
    key_grad,
    logit_grad,
    value_weight_grad,
    output_weight_grad,
    shard,
    chosen,
    sent,
    held,
    relay,
    back_relay,
    banks,
    quarter_bank,
    answer,
    returned,
    gated,
    held_rows,
    wide,
    spread,
    parts,
    pair,
    staged,
    landed,
    back,
    back_in,
    send_x,
    recv_x,
    send_z,
    recv_z,
    send_f,
    recv_f,
    send_p,
    recv_p,
    send_r,
    recv_r,
    local,
):
    tok_rows, features = tokens.shape
    head_size = queries.shape[1]
    experts = gate_logits.shape[0] // 2
    capacity = 5 * tok_rows // (2 * experts)
    half, quarter = features // 2, features // 4
    chips = groups // 2
    shard_rows = features // groups
    block = 4 * capacity
    small = answer.shape[0] // experts
    me_dp = lax.axis_index("dp")
    me_ex = lax.axis_index("expert")
    z, core = me_dp // 2, me_dp % 2
    y, x = me_ex // SIDE, me_ex % SIDE
    partner = z * 2 + 1 - core

    def plane_peer(i):
        return ((y + i // SIDE) % SIDE) * SIDE + (x + i % SIDE) % SIDE

    def chip_step(j):
        return (j % 2) * ((j + 1) // 2) + (1 - j % 2) * (chips - j // 2)

    def chip_peer(j):
        return ((z + chip_step(j)) % chips) * 2 + core

    def chip_source(j):
        return ((z + chips - chip_step(j)) % chips) * 2 + core

    def window(ref, index, size):
        return ref.at[pl.ds(pl.multiple_of(index * size, 16), size)]

    def plane_copy(phase, source, target, size, i):
        peer = plane_peer(i)
        return pltpu.make_async_remote_copy(
            src_ref=window(source, peer, size),
            dst_ref=window(target, me_ex, size),
            send_sem=send_x.at[phase, i],
            recv_sem=recv_x.at[phase, i],
            device_id={"expert": peer},
            device_id_type=MESH,
        )

    def plane_own(phase, source, target, size):
        return pltpu.make_async_copy(
            window(source, me_ex, size), window(target, me_ex, size), local.at[phase]
        )

    def plane_start(phase, source, target, size):
        @pl.loop(1, experts)
        def _(i):
            plane_copy(phase, source, target, size, i).start()

        plane_own(phase, source, target, size).start()

    def plane_wait(phase, source, target, size):
        plane_own(phase, source, target, size).wait()

        @pl.loop(1, experts)
        def _(i):
            plane_copy(phase, source, target, size, i).wait_recv()

    def step(dy, dx):
        return ((y + dy) % SIDE) * SIDE + (x + dx) % SIDE

    def first_leg(phase, source, buffer, size, r):
        (dy, dx), via, _ = RELAYED[r]
        return pltpu.make_async_remote_copy(
            src_ref=window(source, step(dy, dx), size),
            dst_ref=buffer.at[r],
            send_sem=send_x.at[phase, dy * SIDE + dx],
            recv_sem=recv_r.at[phase // 3, r],
            device_id={"expert": step(*via)},
            device_id_type=MESH,
        )

    def last_leg(phase, buffer, target, size, r):
        (dy, dx), via, leg = RELAYED[r]
        return pltpu.make_async_remote_copy(
            src_ref=buffer.at[r],
            dst_ref=window(target, step(SIDE - via[0], SIDE - via[1]), size),
            send_sem=send_r.at[phase // 3, r],
            recv_sem=recv_x.at[phase, dy * SIDE + dx],
            device_id={"expert": step(*leg)},
            device_id_type=MESH,
        )

    direct = [i for i in range(1, SIDE * SIDE) if (i // SIDE, i % SIDE) not in [r[0] for r in RELAYED]]

    def balanced_start(phase, source, buffer, target, size):
        for r in range(len(RELAYED)):
            first_leg(phase, source, buffer, size, r).start()
        for i in sorted(direct, key=lambda i: -(i // SIDE == 2) - (i % SIDE == 2)):
            plane_copy(phase, source, target, size, i).start()
        plane_own(phase, source, target, size).start()

    def balanced_relay(phase, source, buffer, target, size):
        for r in range(len(RELAYED)):
            first_leg(phase, source, buffer, size, r).wait_recv()
            last_leg(phase, buffer, target, size, r).start()

    def balanced_drain(phase, source, buffer, target, size):
        plane_drain(phase, source, target, size)
        for r in range(len(RELAYED)):
            last_leg(phase, buffer, target, size, r).wait_send()

    def plane_drain(phase, source, target, size):
        @pl.loop(1, experts)
        def _(i):
            plane_copy(phase, source, target, size, i).wait_send()

    def shard_copy(j):
        return pltpu.make_async_remote_copy(
            src_ref=shard,
            dst_ref=window(banks, me_dp, shard_rows),
            send_sem=send_z.at[0, j],
            recv_sem=recv_z.at[0, j],
            device_id={"dp": chip_peer(j)},
            device_id_type=MESH,
        )

    def forward_copy(j, source, row):
        return pltpu.make_async_remote_copy(
            src_ref=source,
            dst_ref=window(banks, row, shard_rows),
            send_sem=send_f.at[j],
            recv_sem=recv_f.at[j],
            device_id={"dp": partner},
            device_id_type=MESH,
        )

    def forward_of(j):
        row = chip_source(j)
        return forward_copy(j, window(banks, row, shard_rows), row)

    def sum_copy(j):
        return pltpu.make_async_remote_copy(
            src_ref=staged.at[(z + chip_step(j)) % chips],
            dst_ref=landed.at[z],
            send_sem=send_z.at[1, j],
            recv_sem=recv_z.at[1, j],
            device_id={"dp": chip_peer(j)},
            device_id_type=MESH,
        )

    pair_copy = pltpu.make_async_remote_copy(
        src_ref=parts.at[1 - core],
        dst_ref=pair,
        send_sem=send_p,
        recv_sem=recv_p,
        device_id={"dp": partner},
        device_id_type=MESH,
    )

    barrier = pltpu.get_barrier_semaphore()

    @pl.loop(1, experts)
    def _(i):
        pl.semaphore_signal(barrier, inc=1, device_id={"expert": plane_peer(i)}, device_id_type=MESH)

    @pl.loop(1, chips)
    def _(j):
        pl.semaphore_signal(barrier, inc=1, device_id={"dp": chip_peer(j)}, device_id_type=MESH)

    pl.semaphore_signal(barrier, inc=1, device_id={"dp": partner}, device_id_type=MESH)

    shard[:, :head_size] = value_weight[0]
    shard[:, head_size:] = output_weight[0]
    own_shard = pltpu.make_async_copy(shard, window(banks, me_dp, shard_rows), local.at[4])
    own_shard.start()
    value_stats = route_ranks(value_routes[...], experts)
    output_stats = route_ranks(output_routes[...], experts)
    width = experts * block
    chosen[...] = jnp.concatenate(
        [
            chosen_rows(stats[:2], stats[2:], block, offset, width)
            for stats, offset in (
                (value_stats, 0),
                (output_stats, capacity),
                (value_stats, 2 * capacity),
                (output_stats, 3 * capacity),
            )
        ],
        axis=1,
    )
    reach = chips // 4
    tile = 256
    stripe = SIDE * block

    def stripe_of(index):
        return pl.ds(pl.multiple_of(index * stripe, 16), stripe)

    plane_order = (2, 1, 3, 0)
    for dy in plane_order:
        target_rows = stripe_of((y + dy) % SIDE)
        for c in range(half // tile):
            low = pl.ds(c * tile, tile)
            high = pl.ds(half + c * tile, tile)
            rows = jnp.concatenate(
                [tokens[:, low], cotangent[:, low], tokens[:, high], cotangent[:, high]], axis=0
            )
            sent[target_rows, low] = contract(chosen[target_rows, :], rows, ((1,), (0,))).astype(BF16)
        if dy == plane_order[0]:
            pl.semaphore_wait(barrier, experts - 1 + chips)
            for j in range(2 * reach, 0, -1):
                shard_copy(j).start()
            forward_copy(0, shard, me_dp).start()
        for r in range(len(RELAYED)):
            if RELAYED[r][0][0] == dy:
                first_leg(0, sent, relay, block, r).start()
        for i in direct:
            if i // SIDE == dy:
                plane_copy(0, sent, held, block, i).start()
    plane_own(0, sent, held, block).start()
    columns = jnp.concatenate(value_stats + output_stats, axis=0).T.astype(jnp.int32)
    value_expert, value_place, output_expert, output_place = [
        [columns[:, 2 * n + k : 2 * n + k + 1] for k in range(2)] for n in range(4)
    ]
    expert_ids = lax.broadcasted_iota(jnp.int32, (tok_rows, experts), 1)
    value_hot, output_hot = [
        [jnp.where(expert_ids == column, 1.0, 0.0).astype(F32) for column in pair_of]
        for pair_of in (value_expert, output_expert)
    ]

    def pick_sum(expert, place, stride, offset, width):
        picks = [pick_rows(expert[k], place[k], stride, offset, width) for k in range(2)]
        return (picks[0] + picks[1]).astype(BF16)


    def onward(j, via):
        row = chip_source(via)
        return pltpu.make_async_remote_copy(
            src_ref=window(banks, row, shard_rows),
            dst_ref=window(banks, row, shard_rows),
            send_sem=send_z.at[0, j],
            recv_sem=recv_z.at[0, j],
            device_id={"dp": ((z + chip_step(j) + chips - chip_step(via)) % chips) * 2 + core},
            device_id_type=MESH,
        )

    for via in (2 * reach - 1, 2 * reach):
        shard_copy(via).wait_recv()
        for j in range(2 * reach + 1, chips):
            if j % 2 == via % 2:
                onward(j, via).start()
        forward_of(via).start()

    balanced_relay(0, sent, relay, held, block)

    @pl.loop(1, 2 * reach - 1)
    def _(j):
        shard_copy(j).wait_recv()
        forward_of(j).start()

    @pl.loop(2 * reach + 1, chips)
    def _(j):
        shard_copy(j).wait_recv()
        forward_of(j).start()

    own_shard.wait()

    @pl.loop(0, chips)
    def _(j):
        forward_of(j).wait_recv()

    bank_pair = jnp.concatenate([banks[:half, :], banks[half:, :]], axis=1)
    for q in range(4):
        quarter_bank[:, q * head_size : (q + 1) * head_size] = banks[q * quarter : (q + 1) * quarter, :head_size]

    row_ids = lax.broadcasted_iota(jnp.int32, (2 * capacity, head_size), 0)
    chunk = SIDE
    for dy in plane_order:
        source_y = (y + SIDE - dy) % SIDE
        for dx in range(SIDE):
            if dy or dx:
                plane_copy(0, sent, held, block, dy * SIDE + dx).wait_recv()
            else:
                plane_own(0, sent, held, block).wait()
        both = contract(held[stripe_of(source_y), :], bank_pair, ((1,), (0,)))
        blocks = []
        for k in range(chunk):
            top = both[k * block : k * block + 2 * capacity, : 2 * head_size]
            low = both[k * block + 2 * capacity : (k + 1) * block, 2 * head_size :]
            total = top + low
            rows = jnp.where(row_ids < capacity, total[:, :head_size], total[:, head_size:])
            blocks += [rows, jnp.zeros((small - 2 * capacity, head_size), F32)]
        spot = pl.ds(pl.multiple_of(source_y * SIDE * small, 16), SIDE * small)
        answer[spot, :] = jnp.concatenate(blocks, axis=0).astype(BF16)
        for dx in range(SIDE):
            i = ((SIDE - dy) % SIDE) * SIDE + dx
            if i:
                plane_copy(1, answer, returned, small, i).start()
            else:
                plane_own(1, answer, returned, small).start()

    value_pick = [
        pick_rows(value_expert[k], value_place[k], small, 0, experts * small).astype(BF16) for k in range(2)
    ]
    output_pick = [
        pick_rows(output_expert[k], output_place[k], small, capacity, experts * small).astype(BF16)
        for k in range(2)
    ]
    plane_wait(1, answer, returned, small)
    got = attention_step(
        queries[...],
        key_vectors[...],
        gate_logits[...].T,
        returned[...],
        value_hot,
        output_hot,
        value_pick,
        output_pick,
    )
    gated[...] = got[3]
    plane_start(2, gated, held_rows, small)
    query_grad[...] = got[0]
    key_grad[...] = got[1]
    logit_grad[...] = got[2].T
    out_ids = lax.broadcasted_iota(jnp.int32, (block, small), 0)
    in_ids = lax.broadcasted_iota(jnp.int32, (block, small), 1)
    twice = out_ids - jnp.where(out_ids >= 2 * capacity, 2 * capacity, 0)
    fourfold = twice - jnp.where(twice >= capacity, capacity, 0)
    repeat_two = jnp.where(in_ids == twice, 1.0, 0.0).astype(BF16)
    repeat_four = jnp.where(in_ids == fourfold, 1.0, 0.0).astype(BF16)
    place_ids = lax.broadcasted_iota(jnp.int32, (block, head_size), 0)
    in_quarter = [
        (place_ids >= q * capacity) & (place_ids < (q + 1) * capacity) for q in range(4)
    ]
    plane_wait(2, gated, held_rows, small)
    for e in range(experts):
        rows = held_rows[e * small : (e + 1) * small, :]
        for repeat, target in ((repeat_two, wide), (repeat_four, spread)):
            copies = contract(repeat, rows, ((1,), (0,)))
            target[e * block : (e + 1) * block, :] = jnp.concatenate(
                [jnp.where(mask, copies, 0.0) for mask in in_quarter], axis=1
            ).astype(BF16)

    for c in range(half // tile):
        grads = contract(held[:, c * tile : (c + 1) * tile], wide[...], ((0,), (0,))).astype(BF16)
        for h in range(2):
            for s in range(tile // shard_rows):
                row = (h * half + c * tile) // shard_rows + s
                parts[row % 2, row // 2] = grads[
                    s * shard_rows : (s + 1) * shard_rows, h * 2 * head_size : (h + 1) * 2 * head_size
                ]
    pair_copy.start()
    for c in range(experts // chunk):
        span = slice(c * chunk * block, (c + 1) * chunk * block)
        back[span, :] = contract(spread[span, :], quarter_bank[...], ((1,), (1,))).astype(BF16)
    pair_copy.wait_recv()
    for k in range(chips):
        staged[k] = (parts[core, k].astype(F32) + pair[k].astype(F32)).astype(BF16)

    @pl.loop(1, chips)
    def _(j):
        sum_copy(j).start()

    balanced_start(3, back, back_relay, back_in, block)
    balanced_relay(3, back, back_relay, back_in, block)
    token_pick = [pick_sum(value_expert, value_place, block, q * capacity, width) for q in range(4)]
    plane_wait(3, back, back_in, block)
    for q in range(4):
        token_grad[:, q * quarter : (q + 1) * quarter] = contract(
            token_pick[q], back_in[...], ((1,), (0,))
        ).astype(BF16)

    landed[z] = staged[z]

    @pl.loop(1, chips)
    def _(j):
        sum_copy(j).wait_recv()

    total = landed[0].astype(F32)
    for k in range(1, chips):
        total = total + landed[k].astype(F32)
    total = total / groups
    value_weight_grad[...] = total[:, :head_size]
    output_weight_grad[...] = total[:, head_size:]

    balanced_drain(0, sent, relay, held, block)
    plane_drain(1, answer, returned, small)
    plane_drain(2, gated, held_rows, small)
    balanced_drain(3, back, back_relay, back_in, block)
    pair_copy.wait_send()

    @pl.loop(1, chips)
    def _(j):
        shard_copy(j).wait_send()
        sum_copy(j).wait_send()

    @pl.loop(0, chips)
    def _(j):
        forward_of(j).wait_send()


def hand_over(*refs):
    for source, target in zip(refs[:6], refs[6:]):
        target[...] = source[...]


def on_device(
    tokens,
    queries,
    key_vectors,
    gate_logits,
    value_routes,
    output_routes,
    value_weight,
    output_weight,
    cotangent,
):
    tok_rows, features = tokens.shape
    head_size = queries.shape[1]
    experts = gate_logits.shape[1] // 2
    capacity = 5 * tok_rows // (2 * experts)
    groups = lax.axis_size("dp")
    chips = groups // 2
    shard_rows = features // groups
    small = 48
    block = 4 * capacity
    vmem = pl.BlockSpec(memory_space=pltpu.VMEM)

    def room(*shape):
        return pltpu.VMEM(shape, BF16)

    outs = pl.pallas_call(
        functools.partial(kernel, groups),
        out_shape=(
            jax.ShapeDtypeStruct((tok_rows, features), BF16),
            jax.ShapeDtypeStruct((tok_rows, head_size), BF16),
            jax.ShapeDtypeStruct((tok_rows, head_size), BF16),
            jax.ShapeDtypeStruct((2 * experts, tok_rows), F32),
            jax.ShapeDtypeStruct((shard_rows, head_size), F32),
            jax.ShapeDtypeStruct((shard_rows, head_size), F32),
        ),
        in_specs=[vmem] * 9,
        out_specs=(vmem,) * 6,
        scratch_shapes=[
            room(shard_rows, 2 * head_size),
            room(experts * block, 4 * tok_rows),
            room(experts * block, features // 2),
            room(experts * block, features // 2),
            room(len(RELAYED), block, features // 2),
            room(len(RELAYED), block, features // 4),
            room(features, 2 * head_size),
            room(features // 4, 4 * head_size),
            room(experts * small, head_size),
            room(experts * small, head_size),
            room(experts * small, head_size),
            room(experts * small, head_size),
            room(experts * block, 4 * head_size),
            room(experts * block, 4 * head_size),
            room(2, chips, shard_rows, 2 * head_size),
            room(chips, shard_rows, 2 * head_size),
            room(chips, shard_rows, 2 * head_size),
            room(chips, shard_rows, 2 * head_size),
            room(experts * block, features // 4),
            room(experts * block, features // 4),
            pltpu.SemaphoreType.DMA((4, experts)),
            pltpu.SemaphoreType.DMA((4, experts)),
            pltpu.SemaphoreType.DMA((2, chips)),
            pltpu.SemaphoreType.DMA((2, chips)),
            pltpu.SemaphoreType.DMA((chips,)),
            pltpu.SemaphoreType.DMA((chips,)),
            pltpu.SemaphoreType.DMA,
            pltpu.SemaphoreType.DMA,
            pltpu.SemaphoreType.DMA((2, len(RELAYED))),
            pltpu.SemaphoreType.DMA((2, len(RELAYED))),
            pltpu.SemaphoreType.DMA((5,)),
        ],
        compiler_params=pltpu.CompilerParams(collective_id=0, has_side_effects=True),
    )(
        tokens,
        queries,
        key_vectors,
        gate_logits.T,
        value_routes.T,
        output_routes.T,
        value_weight,
        output_weight,
        cotangent,
    )
    outs = pl.pallas_call(
        hand_over,
        out_shape=tuple(jax.ShapeDtypeStruct(out.shape, out.dtype) for out in outs),
        in_specs=[vmem] * 6,
        out_specs=(vmem,) * 6,
    )(*outs)
    return outs[:3] + (outs[3].T, outs[4][None], outs[5][None])


def solution(mesh):
    rows = P(("dp", "expert"), None)
    bank = P("expert", "dp", None)
    return jax.shard_map(
        on_device,
        mesh=mesh,
        in_specs=(rows,) * 6 + (bank, bank, rows),
        out_specs=(rows,) * 4 + (bank, bank),
        check_vma=False,
    )
```

```python
import functools
import math

import jax
import jax.numpy as jnp
from jax import lax
from jax.experimental import pallas as pl
from jax.experimental.pallas import tpu as pltpu
from jax.sharding import PartitionSpec as P

BF16 = jnp.bfloat16
F32 = jnp.float32
MESH = pl.DeviceIdType.MESH
SIDE = 4
RELAYED = (
    ((1, 2), (0, 3), (1, 3)),
    ((3, 2), (0, 3), (3, 3)),
    ((2, 1), (3, 1), (3, 0)),
    ((2, 3), (3, 3), (3, 0)),
)


def contract(left, right, dims):
    return lax.dot_general(left, right, (dims, ((), ())), preferred_element_type=F32)


def route_ranks(routes, experts):
    tokens = routes.shape[1]
    expert_ids = lax.broadcasted_iota(jnp.int32, (experts, tokens), 0)
    hots = [jnp.where(expert_ids == routes[k : k + 1, :], 1.0, 0.0).astype(F32) for k in range(2)]
    row_ids = lax.broadcasted_iota(jnp.int32, (tokens, tokens), 0)
    col_ids = lax.broadcasted_iota(jnp.int32, (tokens, tokens), 1)
    earlier = jnp.where(row_ids < col_ids, 1.0, 0.0).astype(BF16)
    rank = contract((hots[0] + hots[1]).astype(BF16), earlier, ((1,), (0,)))
    places = [jnp.sum(hot * rank, axis=0, keepdims=True) for hot in hots]
    return [routes[k : k + 1, :].astype(F32) for k in range(2)] + places


def pick_rows(expert, place, stride, offset, width):
    slot_ids = lax.broadcasted_iota(jnp.int32, (expert.shape[0], width), 1)
    return jnp.where(slot_ids == expert * stride + place + offset, 1.0, 0.0).astype(F32)


def chosen_rows(expert, place, stride, offset, width):
    slot_ids = lax.broadcasted_iota(jnp.int32, (width, expert[0].shape[1]), 0)
    slots = [(expert[k] * stride + place[k] + offset).astype(jnp.int32) for k in range(2)]
    return jnp.where((slot_ids == slots[0]) | (slot_ids == slots[1]), 1.0, 0.0).astype(BF16)


def attention_step(queries, keys, gate_logits, returned, value_hot, output_hot, value_pick, output_pick):
    rows, head_size = queries.shape
    experts = gate_logits.shape[1] // 2
    gates = jax.nn.sigmoid(gate_logits)
    value_gate = [jnp.sum(hot * gates[:, :experts], axis=1, keepdims=True) for hot in value_hot]
    output_gate = [jnp.sum(hot * gates[:, experts:], axis=1, keepdims=True) for hot in output_hot]
    expert_value = [contract(pick, returned, ((1,), (0,))) for pick in value_pick]
    head_back = [contract(pick, returned, ((1,), (0,))) for pick in output_pick]
    mixed_value = (value_gate[0] * expert_value[0] + value_gate[1] * expert_value[1]).astype(BF16)
    scores = contract(queries, keys, ((1,), (1,))) / math.sqrt(head_size)
    row_ids = lax.broadcasted_iota(jnp.int32, (rows, rows), 0)
    col_ids = lax.broadcasted_iota(jnp.int32, (rows, rows), 1)
    scores = jnp.where(row_ids >= col_ids, scores, -1e30)
    exponent = jnp.exp(scores - jnp.max(scores, axis=1, keepdims=True))
    probs = exponent / jnp.sum(exponent, axis=1, keepdims=True)
    weights = probs.astype(BF16)
    hidden = contract(weights, mixed_value, ((1,), (0,))).astype(BF16)
    hidden_wide = hidden.astype(F32)
    hidden_grad = (output_gate[0] * head_back[0] + output_gate[1] * head_back[1]).astype(BF16)
    prob_grad = contract(hidden_grad, mixed_value, ((1,), (1,)))
    score_grad = probs * (prob_grad - jnp.sum(prob_grad * probs, axis=1, keepdims=True))
    scaled_grad = (score_grad / math.sqrt(head_size)).astype(BF16)
    query_grad = contract(scaled_grad, keys, ((1,), (0,))).astype(BF16)
    key_grad = contract(scaled_grad, queries, ((0,), (0,))).astype(BF16)
    value_grad = contract(weights, hidden_grad, ((0,), (0,))).astype(BF16)
    value_wide = value_grad.astype(F32)
    gated_value = [(gate * value_wide).astype(BF16) for gate in value_gate]
    gated_hidden = [(gate * hidden_wide).astype(BF16) for gate in output_gate]
    logit_value = 0.0
    logit_output = 0.0
    for k in range(2):
        slope = jnp.sum(value_wide * expert_value[k], axis=1, keepdims=True)
        logit_value += value_hot[k] * (slope * value_gate[k] * (1.0 - value_gate[k]))
        slope = jnp.sum(hidden_wide * head_back[k], axis=1, keepdims=True)
        logit_output += output_hot[k] * (slope * output_gate[k] * (1.0 - output_gate[k]))
    logit_grad = jnp.concatenate([logit_value, logit_output], axis=1)
    sent_rows = contract(
        jnp.concatenate(value_pick + output_pick, axis=0),
        jnp.concatenate(gated_value + gated_hidden, axis=0),
        ((0,), (0,)),
    ).astype(BF16)
    return query_grad, key_grad, logit_grad, sent_rows


def kernel(
    groups,
    tokens,
    queries,
    key_vectors,
    gate_logits,
    value_routes,
    output_routes,
    value_weight,
    output_weight,
    cotangent,
    token_grad,
    query_grad,
    key_grad,
    logit_grad,
    value_weight_grad,
    output_weight_grad,
    shard,
    sent,
    held,
    relay,
    back_relay,
    banks,
    quarter_bank,
    answer,
    returned,
    gated,
    held_rows,
    wide,
    spread,
    parts,
    pair,
    staged,
    landed,
    back,
    back_in,
    send_x,
    recv_x,
    send_z,
    recv_z,
    send_f,
    recv_f,
    send_p,
    recv_p,
    send_r,
    recv_r,
    local,
):
    tok_rows, features = tokens.shape
    head_size = queries.shape[1]
    experts = gate_logits.shape[0] // 2
    capacity = 5 * tok_rows // (2 * experts)
    half, quarter = features // 2, features // 4
    chips = groups // 2
    shard_rows = features // groups
    block = 4 * capacity
    small = answer.shape[0] // experts
    me_dp = lax.axis_index("dp")
    me_ex = lax.axis_index("expert")
    z, core = me_dp // 2, me_dp % 2
    y, x = me_ex // SIDE, me_ex % SIDE
    partner = z * 2 + 1 - core

    def plane_peer(i):
        return ((y + i // SIDE) % SIDE) * SIDE + (x + i % SIDE) % SIDE

    def chip_step(j):
        return (j % 2) * ((j + 1) // 2) + (1 - j % 2) * (chips - j // 2)

    def chip_peer(j):
        return ((z + chip_step(j)) % chips) * 2 + core

    def chip_source(j):
        return ((z + chips - chip_step(j)) % chips) * 2 + core

    def window(ref, index, size):
        return ref.at[pl.ds(pl.multiple_of(index * size, 16), size)]

    def plane_copy(phase, source, target, size, i):
        peer = plane_peer(i)
        return pltpu.make_async_remote_copy(
            src_ref=window(source, peer, size),
            dst_ref=window(target, me_ex, size),
            send_sem=send_x.at[phase, i],
            recv_sem=recv_x.at[phase, i],
            device_id={"expert": peer},
            device_id_type=MESH,
        )

    def plane_own(phase, source, target, size):
        return pltpu.make_async_copy(
            window(source, me_ex, size), window(target, me_ex, size), local.at[phase]
        )

    def plane_start(phase, source, target, size):
        @pl.loop(1, experts)
        def _(i):
            plane_copy(phase, source, target, size, i).start()

        plane_own(phase, source, target, size).start()

    def plane_wait(phase, source, target, size):
        plane_own(phase, source, target, size).wait()

        @pl.loop(1, experts)
        def _(i):
            plane_copy(phase, source, target, size, i).wait_recv()

    def step(dy, dx):
        return ((y + dy) % SIDE) * SIDE + (x + dx) % SIDE

    def first_leg(phase, source, buffer, size, r):
        (dy, dx), via, _ = RELAYED[r]
        return pltpu.make_async_remote_copy(
            src_ref=window(source, step(dy, dx), size),
            dst_ref=buffer.at[r],
            send_sem=send_x.at[phase, dy * SIDE + dx],
            recv_sem=recv_r.at[phase // 3, r],
            device_id={"expert": step(*via)},
            device_id_type=MESH,
        )

    def last_leg(phase, buffer, target, size, r):
        (dy, dx), via, leg = RELAYED[r]
        return pltpu.make_async_remote_copy(
            src_ref=buffer.at[r],
            dst_ref=window(target, step(SIDE - via[0], SIDE - via[1]), size),
            send_sem=send_r.at[phase // 3, r],
            recv_sem=recv_x.at[phase, dy * SIDE + dx],
            device_id={"expert": step(*leg)},
            device_id_type=MESH,
        )

    direct = [i for i in range(1, SIDE * SIDE) if (i // SIDE, i % SIDE) not in [r[0] for r in RELAYED]]

    def balanced_start(phase, source, buffer, target, size):
        for r in range(len(RELAYED)):
            first_leg(phase, source, buffer, size, r).start()
        for i in sorted(direct, key=lambda i: -(i // SIDE == 2) - (i % SIDE == 2)):
            plane_copy(phase, source, target, size, i).start()
        plane_own(phase, source, target, size).start()

    def balanced_relay(phase, source, buffer, target, size):
        for r in range(len(RELAYED)):
            first_leg(phase, source, buffer, size, r).wait_recv()
            last_leg(phase, buffer, target, size, r).start()

    def balanced_drain(phase, source, buffer, target, size):
        plane_drain(phase, source, target, size)
        for r in range(len(RELAYED)):
            last_leg(phase, buffer, target, size, r).wait_send()

    def plane_drain(phase, source, target, size):
        @pl.loop(1, experts)
        def _(i):
            plane_copy(phase, source, target, size, i).wait_send()

    def shard_copy(j):
        return pltpu.make_async_remote_copy(
            src_ref=shard,
            dst_ref=window(banks, me_dp, shard_rows),
            send_sem=send_z.at[0, j],
            recv_sem=recv_z.at[0, j],
            device_id={"dp": chip_peer(j)},
            device_id_type=MESH,
        )

    def forward_copy(j, source, row):
        return pltpu.make_async_remote_copy(
            src_ref=source,
            dst_ref=window(banks, row, shard_rows),
            send_sem=send_f.at[j],
            recv_sem=recv_f.at[j],
            device_id={"dp": partner},
            device_id_type=MESH,
        )

    def forward_of(j):
        row = chip_source(j)
        return forward_copy(j, window(banks, row, shard_rows), row)

    def sum_copy(j):
        return pltpu.make_async_remote_copy(
            src_ref=staged.at[(z + chip_step(j)) % chips],
            dst_ref=landed.at[z],
            send_sem=send_z.at[1, j],
            recv_sem=recv_z.at[1, j],
            device_id={"dp": chip_peer(j)},
            device_id_type=MESH,
        )

    pair_copy = pltpu.make_async_remote_copy(
        src_ref=parts.at[1 - core],
        dst_ref=pair,
        send_sem=send_p,
        recv_sem=recv_p,
        device_id={"dp": partner},
        device_id_type=MESH,
    )

    barrier = pltpu.get_barrier_semaphore()

    @pl.loop(1, experts)
    def _(i):
        pl.semaphore_signal(barrier, inc=1, device_id={"expert": plane_peer(i)}, device_id_type=MESH)

    @pl.loop(1, chips)
    def _(j):
        pl.semaphore_signal(barrier, inc=1, device_id={"dp": chip_peer(j)}, device_id_type=MESH)

    pl.semaphore_signal(barrier, inc=1, device_id={"dp": partner}, device_id_type=MESH)

    shard[:, :head_size] = value_weight[0]
    shard[:, head_size:] = output_weight[0]
    own_shard = pltpu.make_async_copy(shard, window(banks, me_dp, shard_rows), local.at[4])
    own_shard.start()
    value_stats = route_ranks(value_routes[...], experts)
    output_stats = route_ranks(output_routes[...], experts)
    width = experts * block
    chosen = jnp.concatenate(
        [
            chosen_rows(stats[:2], stats[2:], block, offset, width)
            for stats, offset in (
                (value_stats, 0),
                (output_stats, capacity),
                (value_stats, 2 * capacity),
                (output_stats, 3 * capacity),
            )
        ],
        axis=1,
    )
    tile = 256
    cut = width // 2
    for c in range(half // tile):
        low = pl.ds(c * tile, tile)
        high = pl.ds(half + c * tile, tile)
        rows = jnp.concatenate([tokens[:, low], cotangent[:, low], tokens[:, high], cotangent[:, high]], axis=0)
        for part in range(2):
            sent[part * cut : (part + 1) * cut, low] = contract(
                chosen[part * cut : (part + 1) * cut, :], rows, ((1,), (0,))
            ).astype(BF16)

    pl.semaphore_wait(barrier, experts - 1 + chips)
    reach = chips // 4
    for j in range(2 * reach, 0, -1):
        shard_copy(j).start()
    balanced_start(0, sent, relay, held, block)

    forward_copy(0, shard, me_dp).start()
    columns = jnp.concatenate(value_stats + output_stats, axis=0).T.astype(jnp.int32)
    value_expert, value_place, output_expert, output_place = [
        [columns[:, 2 * n + k : 2 * n + k + 1] for k in range(2)] for n in range(4)
    ]
    expert_ids = lax.broadcasted_iota(jnp.int32, (tok_rows, experts), 1)
    value_hot, output_hot = [
        [jnp.where(expert_ids == column, 1.0, 0.0).astype(F32) for column in pair_of]
        for pair_of in (value_expert, output_expert)
    ]

    def pick_sum(expert, place, stride, offset, width):
        picks = [pick_rows(expert[k], place[k], stride, offset, width) for k in range(2)]
        return (picks[0] + picks[1]).astype(BF16)

    def onward(j, via):
        row = chip_source(via)
        return pltpu.make_async_remote_copy(
            src_ref=window(banks, row, shard_rows),
            dst_ref=window(banks, row, shard_rows),
            send_sem=send_z.at[0, j],
            recv_sem=recv_z.at[0, j],
            device_id={"dp": ((z + chip_step(j) + chips - chip_step(via)) % chips) * 2 + core},
            device_id_type=MESH,
        )

    for via in (2 * reach - 1, 2 * reach):
        shard_copy(via).wait_recv()
        for j in range(2 * reach + 1, chips):
            if j % 2 == via % 2:
                onward(j, via).start()
        forward_of(via).start()

    balanced_relay(0, sent, relay, held, block)

    @pl.loop(1, 2 * reach - 1)
    def _(j):
        shard_copy(j).wait_recv()
        forward_of(j).start()

    @pl.loop(2 * reach + 1, chips)
    def _(j):
        shard_copy(j).wait_recv()
        forward_of(j).start()

    own_shard.wait()

    @pl.loop(0, chips)
    def _(j):
        forward_of(j).wait_recv()

    bank_pair = jnp.concatenate([banks[:half, :], banks[half:, :]], axis=1)
    for q in range(4):
        quarter_bank[:, q * head_size : (q + 1) * head_size] = banks[q * quarter : (q + 1) * quarter, :head_size]

    plane_wait(0, sent, held, block)

    row_ids = lax.broadcasted_iota(jnp.int32, (2 * capacity, head_size), 0)
    chunk = 4
    for c in range(experts // chunk):
        both = contract(held[c * chunk * block : (c + 1) * chunk * block, :], bank_pair, ((1,), (0,)))
        for k in range(chunk):
            top = both[k * block : k * block + 2 * capacity, : 2 * head_size]
            low = both[k * block + 2 * capacity : (k + 1) * block, 2 * head_size :]
            total = top + low
            rows = jnp.where(row_ids < capacity, total[:, :head_size], total[:, head_size:])
            rows = jnp.concatenate([rows, jnp.zeros((small - 2 * capacity, head_size), F32)], axis=0)
            e = c * chunk + k
            answer[e * small : (e + 1) * small, :] = rows.astype(BF16)

    plane_start(1, answer, returned, small)
    value_pick = [
        pick_rows(value_expert[k], value_place[k], small, 0, experts * small).astype(BF16) for k in range(2)
    ]
    output_pick = [
        pick_rows(output_expert[k], output_place[k], small, capacity, experts * small).astype(BF16)
        for k in range(2)
    ]
    plane_wait(1, answer, returned, small)
    got = attention_step(
        queries[...],
        key_vectors[...],
        gate_logits[...].T,
        returned[...],
        value_hot,
        output_hot,
        value_pick,
        output_pick,
    )
    gated[...] = got[3]
    plane_start(2, gated, held_rows, small)
    query_grad[...] = got[0]
    key_grad[...] = got[1]
    logit_grad[...] = got[2].T
    out_ids = lax.broadcasted_iota(jnp.int32, (block, small), 0)
    in_ids = lax.broadcasted_iota(jnp.int32, (block, small), 1)
    twice = out_ids - jnp.where(out_ids >= 2 * capacity, 2 * capacity, 0)
    fourfold = twice - jnp.where(twice >= capacity, capacity, 0)
    repeat_two = jnp.where(in_ids == twice, 1.0, 0.0).astype(BF16)
    repeat_four = jnp.where(in_ids == fourfold, 1.0, 0.0).astype(BF16)
    place_ids = lax.broadcasted_iota(jnp.int32, (block, head_size), 0)
    in_quarter = [
        (place_ids >= q * capacity) & (place_ids < (q + 1) * capacity) for q in range(4)
    ]
    plane_wait(2, gated, held_rows, small)
    for e in range(experts):
        rows = held_rows[e * small : (e + 1) * small, :]
        for repeat, target in ((repeat_two, wide), (repeat_four, spread)):
            copies = contract(repeat, rows, ((1,), (0,)))
            target[e * block : (e + 1) * block, :] = jnp.concatenate(
                [jnp.where(mask, copies, 0.0) for mask in in_quarter], axis=1
            ).astype(BF16)

    for c in range(half // tile):
        grads = contract(held[:, c * tile : (c + 1) * tile], wide[...], ((0,), (0,))).astype(BF16)
        for h in range(2):
            for s in range(tile // shard_rows):
                row = (h * half + c * tile) // shard_rows + s
                parts[row % 2, row // 2] = grads[
                    s * shard_rows : (s + 1) * shard_rows, h * 2 * head_size : (h + 1) * 2 * head_size
                ]
    pair_copy.start()
    for c in range(experts // chunk):
        span = slice(c * chunk * block, (c + 1) * chunk * block)
        back[span, :] = contract(spread[span, :], quarter_bank[...], ((1,), (1,))).astype(BF16)
    pair_copy.wait_recv()
    for k in range(chips):
        staged[k] = (parts[core, k].astype(F32) + pair[k].astype(F32)).astype(BF16)

    @pl.loop(1, chips)
    def _(j):
        sum_copy(j).start()

    balanced_start(3, back, back_relay, back_in, block)
    balanced_relay(3, back, back_relay, back_in, block)
    token_pick = [pick_sum(value_expert, value_place, block, q * capacity, width) for q in range(4)]
    plane_wait(3, back, back_in, block)
    for q in range(4):
        token_grad[:, q * quarter : (q + 1) * quarter] = contract(
            token_pick[q], back_in[...], ((1,), (0,))
        ).astype(BF16)

    landed[z] = staged[z]

    @pl.loop(1, chips)
    def _(j):
        sum_copy(j).wait_recv()

    total = landed[0].astype(F32)
    for k in range(1, chips):
        total = total + landed[k].astype(F32)
    total = total / groups
    value_weight_grad[...] = total[:, :head_size]
    output_weight_grad[...] = total[:, head_size:]

    balanced_drain(0, sent, relay, held, block)
    plane_drain(1, answer, returned, small)
    plane_drain(2, gated, held_rows, small)
    balanced_drain(3, back, back_relay, back_in, block)
    pair_copy.wait_send()

    @pl.loop(1, chips)
    def _(j):
        shard_copy(j).wait_send()
        sum_copy(j).wait_send()

    @pl.loop(0, chips)
    def _(j):
        forward_of(j).wait_send()


def hand_over(*refs):
    for source, target in zip(refs[:6], refs[6:]):
        target[...] = source[...]


def on_device(
    tokens,
    queries,
    key_vectors,
    gate_logits,
    value_routes,
    output_routes,
    value_weight,
    output_weight,
    cotangent,
):
    tok_rows, features = tokens.shape
    head_size = queries.shape[1]
    experts = gate_logits.shape[1] // 2
    capacity = 5 * tok_rows // (2 * experts)
    groups = lax.axis_size("dp")
    chips = groups // 2
    shard_rows = features // groups
    small = 48
    block = 4 * capacity
    vmem = pl.BlockSpec(memory_space=pltpu.VMEM)

    def room(*shape):
        return pltpu.VMEM(shape, BF16)

    outs = pl.pallas_call(
        functools.partial(kernel, groups),
        out_shape=(
            jax.ShapeDtypeStruct((tok_rows, features), BF16),
            jax.ShapeDtypeStruct((tok_rows, head_size), BF16),
            jax.ShapeDtypeStruct((tok_rows, head_size), BF16),
            jax.ShapeDtypeStruct((2 * experts, tok_rows), F32),
            jax.ShapeDtypeStruct((shard_rows, head_size), F32),
            jax.ShapeDtypeStruct((shard_rows, head_size), F32),
        ),
        in_specs=[vmem] * 9,
        out_specs=(vmem,) * 6,
        scratch_shapes=[
            room(shard_rows, 2 * head_size),
            room(experts * block, features // 2),
            room(experts * block, features // 2),
            room(len(RELAYED), block, features // 2),
            room(len(RELAYED), block, features // 4),
            room(features, 2 * head_size),
            room(features // 4, 4 * head_size),
            room(experts * small, head_size),
            room(experts * small, head_size),
            room(experts * small, head_size),
            room(experts * small, head_size),
            room(experts * block, 4 * head_size),
            room(experts * block, 4 * head_size),
            room(2, chips, shard_rows, 2 * head_size),
            room(chips, shard_rows, 2 * head_size),
            room(chips, shard_rows, 2 * head_size),
            room(chips, shard_rows, 2 * head_size),
            room(experts * block, features // 4),
            room(experts * block, features // 4),
            pltpu.SemaphoreType.DMA((4, experts)),
            pltpu.SemaphoreType.DMA((4, experts)),
            pltpu.SemaphoreType.DMA((2, chips)),
            pltpu.SemaphoreType.DMA((2, chips)),
            pltpu.SemaphoreType.DMA((chips,)),
            pltpu.SemaphoreType.DMA((chips,)),
            pltpu.SemaphoreType.DMA,
            pltpu.SemaphoreType.DMA,
            pltpu.SemaphoreType.DMA((2, len(RELAYED))),
            pltpu.SemaphoreType.DMA((2, len(RELAYED))),
            pltpu.SemaphoreType.DMA((5,)),
        ],
        compiler_params=pltpu.CompilerParams(collective_id=0, has_side_effects=True),
    )(
        tokens,
        queries,
        key_vectors,
        gate_logits.T,
        value_routes.T,
        output_routes.T,
        value_weight,
        output_weight,
        cotangent,
    )
    outs = pl.pallas_call(
        hand_over,
        out_shape=tuple(jax.ShapeDtypeStruct(out.shape, out.dtype) for out in outs),
        in_specs=[vmem] * 6,
        out_specs=(vmem,) * 6,
    )(*outs)
    return outs[:3] + (outs[3].T, outs[4][None], outs[5][None])


def solution(mesh):
    rows = P(("dp", "expert"), None)
    bank = P("expert", "dp", None)
    return jax.shard_map(
        on_device,
        mesh=mesh,
        in_specs=(rows,) * 6 + (bank, bank, rows),
        out_specs=(rows,) * 4 + (bank, bank),
        check_vma=False,
    )
```
